32 devices in a mesh: dp: 16 (over z, x, core), tensor: 2 (over y).
Axes of the slice: x: 2, y: 2, z: 4, core: 2. Of those that a mesh axis runs over, the one named last changes fastest.
Arguments:
- tokens: bfloat16 [16384, 1024], P(('dp', 'tensor')), may hold values from -6 to 6
- cotangent: bfloat16 [16384, 1024], P(('dp', 'tensor')), may hold values from -6 to 6
- lengths: int32 [16, 4], P('dp'), may hold values from 1 to 512, 1024 in all within a row
- w_in: bfloat16 [1024, 3, 1024], P('dp', None, 'tensor'), may hold values from -0.1875 to 0.1875
- w_out: bfloat16 [1024, 1024], P('tensor', 'dp'), may hold values from -0.1875 to 0.1875
- w_gate_up: bfloat16 [1024, 2, 4608], P('dp', None, 'tensor'), may hold values from -0.1875 to 0.1875
- w_down: bfloat16 [4608, 1024], P('tensor', 'dp'), may hold values from -0.1875 to 0.1875
- conv_weight: float32 [3, 1024], P(None, 'tensor'), may hold values from -3 to 3
- norm_gains: float32 [2, 1024], replicated, may hold values from 0.1 to 1.9
Outputs:
- block_out: bfloat16 [16384, 1024], P(('dp', 'tensor'))
- grad_tokens: bfloat16 [16384, 1024], P(('dp', 'tensor'))
- grad_w_in: float32 [1024, 3, 1024], P('dp', None, 'tensor')
- grad_w_out: float32 [1024, 1024], P('tensor', 'dp')
- grad_w_gate_up: float32 [1024, 2, 4608], P('dp', None, 'tensor')
- grad_w_down: float32 [4608, 1024], P('tensor', 'dp')
- grad_conv_weight: float32 [3, 1024], P(None, 'tensor')
- grad_norm_gains: float32 [2, 1024], replicated
The draws below stay inside these ranges and needn't reach their ends.
Inputs may be any that keep to these rules, and one draw needn't show every extreme that they name: Each row of lengths sums to 1024, and its largest entry is exactly 512.
All inputs are finite; a program needn't handle non-finite values.
Results may differ from the reference program's by a relative error of at most 0.015.
Values may be sent and summed in bfloat16 or wider, within the bound.
A program may use at most 192 MiB of HBM per device.

```python
import math
import jax
import jax.numpy as jnp
import numpy as np
from jax import lax

D = 1024
FF = 4608
TAPS = 3
MAXLEN = 512
ROWS_DP = 1024
SEQS = 4
TOKENS = 16384
N_DP = 16


def levels(rng, extent, cuts, least, top_value):
    factor_of = 1.0
    for dim, blocks in cuts:
        draws = jax.random.uniform(jax.random.fold_in(jax.random.fold_in(rng, 6), dim), (blocks,), jnp.float32, least / len(cuts), top_value / len(cuts))
        factor_of = factor_of * jnp.repeat(jnp.exp(draws), extent[dim] // blocks).reshape((-1,) + (1,) * (len(extent) - 1 - dim))
    return factor_of


def length_profile(amount, total, bound, skew):
    weights = [(1 << 20) // math.isqrt(rank ** skew) + 1 for rank in range(2, amount + 1)]
    surplus, holding = total - bound - (amount - 1), [1] * (amount - 1)
    while surplus > 0:
        movable = [i for i in range(amount - 1) if holding[i] < bound]
        whole, budget = sum([weights[i] for i in movable]), surplus
        for i in movable:
            addition = min(bound - holding[i], max(1, budget * weights[i] // whole), surplus)
            holding[i] = holding[i] + addition
            surplus = surplus - addition
    return np.array([bound] + holding)


def uneven(own_key, number_of, total, reach, lean):
    if number_of == 2:
        one = jax.random.randint(own_key, (), max(1, total - reach), min(reach, total - 1) + 1)
        return jnp.stack([one, total - one])
    sizes = jnp.asarray(length_profile(number_of, total, reach, lean), jnp.int32)
    couples = (number_of - 1) // 2
    giver, receiver = sizes[1:1 + 2 * couples:2], sizes[2:2 + 2 * couples:2]
    slack = jnp.minimum(giver - 1, reach - receiver)
    moved = jax.random.randint(jax.random.fold_in(own_key, 1), (couples,), 0, 1 << 20) % (slack + 1)
    sizes = sizes.at[1:1 + 2 * couples:2].set(giver - moved).at[2:2 + 2 * couples:2].set(receiver + moved)
    return sizes[jax.random.permutation(jax.random.fold_in(own_key, 2), number_of)]


def scatter_about(own_key, dims, deviation, limit, shards=(), kind=jnp.bfloat16):
    result = deviation * jax.random.normal(own_key, dims, jnp.float32)
    if shards:
        result = result * levels(own_key, dims, shards, -0.22, 0.18)
    return jnp.clip(result, -limit, limit).astype(kind)


def setup_inputs(seed: int = 0) -> dict:
    key_of = jax.random.split(jax.random.key(seed), 10)
    return {
        "tokens": scatter_about(key_of[0], (TOKENS, D), 1.0, 6.0, ((0, 32),)),
        "cotangent": scatter_about(key_of[1], (TOKENS, D), 1.0, 6.0, ((0, 32),)),
        "lengths": jax.vmap(lambda own: uneven(own, SEQS, ROWS_DP, MAXLEN, 2))(jax.random.split(key_of[2], N_DP)).reshape((N_DP, SEQS)).astype(jnp.int32),
        "w_in": scatter_about(key_of[3], (D, 3, D), D ** -0.5, 0.1875, ((0, 16), (2, 2))),
        "w_out": scatter_about(key_of[4], (D, D), D ** -0.5, 0.1875, ((0, 2), (1, 16))),
        "w_gate_up": scatter_about(key_of[5], (D, 2, FF), D ** -0.5, 0.1875, ((0, 16), (2, 2))),
        "w_down": scatter_about(key_of[6], (FF, D), (FF // 4) ** -0.5, 0.1875, ((0, 2), (1, 16))),
        "conv_weight": scatter_about(key_of[7], (TAPS, D), 0.6, 3.0, ((1, 2),), jnp.float32),
        "norm_gains": jnp.clip(1.0 + 0.18 * jax.random.normal(key_of[8], (2, D), jnp.float32), 0.1, 1.9),
    }


epsilon = 1e-05

def positions(seq_lengths, row_count):
    seq_lengths = seq_lengths.astype(jnp.int32)
    starts = (jnp.cumsum(seq_lengths) - seq_lengths).astype(jnp.int32)
    row_index = jnp.arange(row_count, dtype=jnp.int32)
    begun_at = jnp.where(starts[None, :] <= row_index[:, None], starts[None, :], jnp.int32(0))
    return (row_index - lax.optimization_barrier(jnp.max(begun_at, axis=1))).astype(jnp.int32)

def delayed(values, steps):
    return jnp.concatenate([jnp.zeros((steps, values.shape[1]), values.dtype), values[:-steps]], 0)

def advanced(values, steps):
    return jnp.concatenate([values[steps:], jnp.zeros((steps, values.shape[1]), values.dtype)], 0)

def one_group(x_rows, cot_rows, seq_lengths, w_in, w_out, w_gate_up, w_down, conv_weight, norm_gains):
    row_count = x_rows.shape[0]
    position = positions(seq_lengths, row_count)
    first_keep = (position >= 1).astype(jnp.float32)[:, None]
    second_keep = (position >= 2).astype(jnp.float32)[:, None]
    x_float = x_rows.astype(jnp.float32)
    rms_first = lax.rsqrt(lax.optimization_barrier(jnp.mean(x_float * x_float, axis=1, keepdims=True)) + epsilon)
    normed_first = (x_float * rms_first * norm_gains[0]).astype(jnp.bfloat16)
    flat_in = w_in.reshape(D, 3 * D)
    projected = jnp.dot(normed_first, flat_in, preferred_element_type=jnp.float32)
    proj_b = projected[:, :D]
    proj_c = projected[:, D:2 * D]
    proj_x = projected[:, 2 * D:]
    gated_in = proj_b * proj_x
    conv_out = conv_weight[0] * gated_in + conv_weight[1] * delayed(gated_in, 1) * first_keep + conv_weight[2] * delayed(gated_in, 2) * second_keep
    mixer_in = (proj_c * conv_out).astype(jnp.bfloat16)
    residual_mid = x_float + jnp.dot(mixer_in, w_out, preferred_element_type=jnp.float32)
    rms_second = lax.rsqrt(lax.optimization_barrier(jnp.mean(residual_mid * residual_mid, axis=1, keepdims=True)) + epsilon)
    normed_second = (residual_mid * rms_second * norm_gains[1]).astype(jnp.bfloat16)
    flat_gu = w_gate_up.reshape(D, 2 * FF)
    gate_up = jnp.dot(normed_second, flat_gu, preferred_element_type=jnp.float32)
    gate_pre = gate_up[:, :FF]
    up_pre = gate_up[:, FF:]
    sig_gate = jax.nn.sigmoid(gate_pre)
    hidden_act = (gate_pre * sig_gate * up_pre).astype(jnp.bfloat16)
    block_out = (residual_mid + jnp.dot(hidden_act, w_down, preferred_element_type=jnp.float32)).astype(jnp.bfloat16)
    grad_act = jnp.dot(cot_rows, w_down.T, preferred_element_type=jnp.float32)
    grad_down = jnp.dot(hidden_act.T, cot_rows, preferred_element_type=jnp.float32)
    grad_gate = (grad_act * up_pre * sig_gate * (1.0 + gate_pre * (1.0 - sig_gate))).astype(jnp.bfloat16)
    grad_up = (grad_act * gate_pre * sig_gate).astype(jnp.bfloat16)
    grad_hidden = jnp.concatenate([grad_gate, grad_up], 1)
    grad_gu = jnp.dot(normed_second.T, grad_hidden, preferred_element_type=jnp.float32).reshape(D, 2, FF)
    grad_normed2 = jnp.dot(grad_hidden, flat_gu.T, preferred_element_type=jnp.float32)
    scaled_two = grad_normed2 * norm_gains[1]
    grad_mid = cot_rows.astype(jnp.float32) + rms_second * scaled_two - residual_mid * (rms_second * rms_second * rms_second) * lax.optimization_barrier(jnp.mean(scaled_two * residual_mid, axis=1, keepdims=True))
    gain_two = lax.optimization_barrier(jnp.sum(grad_normed2 * residual_mid * rms_second, axis=0))
    grad_mid_b = grad_mid.astype(jnp.bfloat16)
    grad_mixer_in = jnp.dot(grad_mid_b, w_out.T, preferred_element_type=jnp.float32)
    grad_wout = jnp.dot(mixer_in.T, grad_mid_b, preferred_element_type=jnp.float32)
    grad_conv_out = grad_mixer_in * proj_c
    grad_gated = conv_weight[0] * grad_conv_out + conv_weight[1] * advanced(grad_conv_out * first_keep, 1) + conv_weight[2] * advanced(grad_conv_out * second_keep, 2)
    grad_taps = jnp.stack([lax.optimization_barrier(jnp.sum(grad_conv_out * gated_in, axis=0)), lax.optimization_barrier(jnp.sum(grad_conv_out * first_keep * delayed(gated_in, 1), axis=0)), lax.optimization_barrier(jnp.sum(grad_conv_out * second_keep * delayed(gated_in, 2), axis=0))])
    grad_proj = jnp.concatenate([grad_gated * proj_x, grad_mixer_in * conv_out, grad_gated * proj_b], 1).astype(jnp.bfloat16)
    grad_win = jnp.dot(normed_first.T, grad_proj, preferred_element_type=jnp.float32).reshape(D, 3, D)
    grad_normed1 = jnp.dot(grad_proj, flat_in.T, preferred_element_type=jnp.float32)
    scaled_one = grad_normed1 * norm_gains[0]
    grad_tokens = (grad_mid + rms_first * scaled_one - x_float * (rms_first * rms_first * rms_first) * lax.optimization_barrier(jnp.mean(scaled_one * x_float, axis=1, keepdims=True))).astype(jnp.bfloat16)
    gain_one = lax.optimization_barrier(jnp.sum(grad_normed1 * x_float * rms_first, axis=0))
    grads = (grad_win, grad_wout, grad_gu, grad_down, grad_taps, jnp.stack([gain_one, gain_two]))
    return (block_out, grad_tokens, grads)

def reference(tokens, cotangent, lengths, w_in, w_out, w_gate_up, w_down, conv_weight, norm_gains):
    x_groups = tokens.reshape(N_DP, ROWS_DP, D)
    cot_groups = cotangent.reshape(N_DP, ROWS_DP, D)
    initial = (jnp.zeros((D, 3, D), jnp.float32), jnp.zeros((D, D), jnp.float32), jnp.zeros((D, 2, FF), jnp.float32), jnp.zeros((FF, D), jnp.float32), jnp.zeros((TAPS, D), jnp.float32), jnp.zeros((2, D), jnp.float32))

    def step_group(totals, inputs):
        x_rows, cot_rows, seq_lengths = inputs
        block_out, grad_tokens, grads = one_group(x_rows, cot_rows, seq_lengths, w_in, w_out, w_gate_up, w_down, conv_weight, norm_gains)
        totals = tuple((total + grad for total, grad in zip(totals, grads)))
        return (totals, (block_out, grad_tokens))
    totals, stacked = lax.scan(step_group, initial, (x_groups, cot_groups, lengths))
    block_out = stacked[0].reshape(TOKENS, D)
    grad_tokens = stacked[1].reshape(TOKENS, D)
    return (block_out, grad_tokens, totals[0], totals[1], totals[2], totals[3], totals[4], totals[5])
```

```python
import functools

import jax
import jax.numpy as jnp
from jax import lax
from jax.experimental import pallas as pl
from jax.experimental.pallas import tpu as pltpu
from jax.sharding import PartitionSpec as P

epsilon = 1e-05


def sequence_starts(seq_lengths):
    count = seq_lengths.shape[0]
    before = jnp.arange(count)[None, :] < jnp.arange(count)[:, None]
    return jnp.sum(jnp.where(before, seq_lengths[None, :], 0), axis=1)


def positions(seq_lengths, row_count):
    starts = sequence_starts(seq_lengths)
    row_index = jnp.arange(row_count, dtype=jnp.int32)
    begun_at = jnp.where(starts[None, :] <= row_index[:, None], starts[None, :], jnp.int32(0))
    return row_index - jnp.max(begun_at, axis=1)


def delayed(values, steps):
    return jnp.concatenate([jnp.zeros((steps, values.shape[1]), values.dtype), values[:-steps]], 0)


def advanced(values, steps):
    return jnp.concatenate([values[steps:], jnp.zeros((steps, values.shape[1]), values.dtype)], 0)


def gather_rows(values):
    count = lax.axis_size("tensor")
    if count != 2:
        return lax.all_gather(values, "tensor", axis=0, tiled=True)
    rows = values.shape[0]
    index = lax.axis_index("tensor")
    other = lax.ppermute(values, "tensor", [(0, 1), (1, 0)])
    whole = jnp.zeros((2 * rows, values.shape[1]), values.dtype)
    whole = lax.dynamic_update_slice_in_dim(whole, values, index * rows, 0)
    return lax.dynamic_update_slice_in_dim(whole, other, (1 - index) * rows, 0)


def scatter_rows(values):
    count = lax.axis_size("tensor")
    if count != 2:
        return lax.psum_scatter(
            values.astype(jnp.bfloat16), "tensor", scatter_dimension=0, tiled=True
        ).astype(jnp.float32)
    rows = values.shape[0] // 2
    index = lax.axis_index("tensor")
    away = lax.dynamic_slice_in_dim(values, (1 - index) * rows, rows, 0).astype(jnp.bfloat16)
    other = lax.ppermute(away, "tensor", [(0, 1), (1, 0)])
    return lax.dynamic_slice_in_dim(values, index * rows, rows, 0) + other.astype(jnp.float32)


def butterfly_sum(values, axis):
    count = lax.axis_size(axis)
    if count & (count - 1):
        return lax.psum(values, axis)
    step = 1
    while step < count:
        values = values + lax.ppermute(values, axis, [(i, i ^ step) for i in range(count)])
        step *= 2
    return values


def gather_blocks(shard, axis):
    count = lax.axis_size(axis)
    if count & (count - 1):
        return lax.all_gather(shard, axis, axis=0, tiled=True)
    index = lax.axis_index(axis)
    blocks = shard[None]
    step = count // 2
    while step >= 1:
        other = lax.ppermute(blocks, axis, [(i, i ^ step) for i in range(count)])
        upper = (index // step) % 2 == 1
        first = jnp.where(upper, other, blocks)
        second = jnp.where(upper, blocks, other)
        blocks = jnp.stack([first, second], axis=1).reshape((-1,) + shard.shape)
        step //= 2
    return blocks.reshape((-1,) + shard.shape[1:])


def scatter_blocks(values, axis):
    count = lax.axis_size(axis)
    if count & (count - 1):
        return lax.psum_scatter(values, axis, scatter_dimension=0, tiled=True)
    index = lax.axis_index(axis)
    shape = (values.shape[0] // count,) + values.shape[1:]
    step = 1
    while step < count:
        pairs = values.reshape((count // step // 2, 2) + shape)
        side = (index // step) % 2
        away = lax.dynamic_index_in_dim(pairs, 1 - side, 1, keepdims=False)
        kept = lax.dynamic_index_in_dim(pairs, side, 1, keepdims=False)
        other = lax.ppermute(away, axis, [(i, i ^ step) for i in range(count)])
        values = (kept.astype(jnp.float32) + other.astype(jnp.float32)).astype(values.dtype)
        step *= 2
    return values.reshape(shape)


def body(tokens, cotangent, lengths, w_in, w_out, w_gate_up, w_down, conv_weight, norm_gains):
    shard_rows, taken, chan_count = w_in.shape
    hidden = w_gate_up.shape[2]
    packed = jnp.concatenate([w_in.reshape(shard_rows, taken * chan_count), w_out.T], axis=1)
    full_mix = lax.all_gather(packed, "dp", axis=0, tiled=True)
    full_gu = lax.all_gather(
        w_gate_up.reshape(shard_rows, 2 * hidden), "dp", axis=0, tiled=True
    )
    full_down = gather_blocks(w_down.T, "dp")
    full_in = full_mix[:, : taken * chan_count]
    full_out = full_mix[:, taken * chan_count :]
    x_float = tokens.astype(jnp.float32)
    rms_first = lax.rsqrt(jnp.mean(x_float * x_float, axis=1, keepdims=True) + epsilon)
    normed_first = (x_float * rms_first * norm_gains[0]).astype(jnp.bfloat16)
    first_all = gather_rows(normed_first)
    cot_all = gather_rows(cotangent)
    row_count = first_all.shape[0]
    position = positions(lengths[0], row_count)
    first_keep = (position >= 1).astype(jnp.float32)[:, None]
    second_keep = (position >= 2).astype(jnp.float32)[:, None]
    projected = jnp.dot(first_all, full_in, preferred_element_type=jnp.float32)
    proj_b = projected[:, :chan_count]
    proj_c = projected[:, chan_count : 2 * chan_count]
    proj_x = projected[:, 2 * chan_count :]
    gated_in = proj_b * proj_x
    conv_out = (
        conv_weight[0] * gated_in
        + conv_weight[1] * delayed(gated_in, 1) * first_keep
        + conv_weight[2] * delayed(gated_in, 2) * second_keep
    )
    mixer_in = (proj_c * conv_out).astype(jnp.bfloat16)
    residual_mid = x_float + scatter_rows(
        jnp.einsum("rc,dc->rd", mixer_in, full_out, preferred_element_type=jnp.float32)
    )
    rms_second = lax.rsqrt(jnp.mean(residual_mid * residual_mid, axis=1, keepdims=True) + epsilon)
    normed_second = (residual_mid * rms_second * norm_gains[1]).astype(jnp.bfloat16)
    second_all = gather_rows(normed_second)
    gate_up = jnp.dot(second_all, full_gu, preferred_element_type=jnp.float32)
    gate_pre = gate_up[:, :hidden]
    up_pre = gate_up[:, hidden:]
    sig_gate = jax.nn.sigmoid(gate_pre)
    hidden_act = (gate_pre * sig_gate * up_pre).astype(jnp.bfloat16)
    grad_down = jnp.einsum("rd,rf->df", cot_all, hidden_act, preferred_element_type=jnp.float32)
    grad_down, full_down = lax.optimization_barrier((grad_down.astype(jnp.bfloat16), full_down))
    sum_down = lax.psum_scatter(grad_down, "dp", scatter_dimension=0, tiled=True)
    grad_act = jnp.einsum("rd,df->rf", cot_all, full_down, preferred_element_type=jnp.float32)
    grad_gate = (grad_act * up_pre * sig_gate * (1.0 + gate_pre * (1.0 - sig_gate))).astype(
        jnp.bfloat16
    )
    grad_up = (grad_act * gate_pre * sig_gate).astype(jnp.bfloat16)
    grad_hidden = jnp.concatenate([grad_gate, grad_up], axis=1)
    grad_gu = jnp.einsum("rd,rf->df", second_all, grad_hidden, preferred_element_type=jnp.float32)
    grad_gu, grad_gate, grad_up = lax.optimization_barrier(
        (grad_gu.astype(jnp.bfloat16), grad_gate, grad_up)
    )
    grad_hidden = jnp.concatenate([grad_gate, grad_up], axis=1)
    grad_gu, sum_down = lax.optimization_barrier((grad_gu, sum_down))
    sum_gu = lax.psum_scatter(grad_gu, "dp", scatter_dimension=0, tiled=True)
    grad_normed2 = scatter_rows(
        jnp.einsum("rf,df->rd", grad_hidden, full_gu, preferred_element_type=jnp.float32)
    )
    block_out = (
        residual_mid
        + scatter_rows(
            jnp.einsum("rf,df->rd", hidden_act, full_down, preferred_element_type=jnp.float32)
        )
    ).astype(jnp.bfloat16)
    scaled_two = grad_normed2 * norm_gains[1]
    grad_mid = (
        cotangent.astype(jnp.float32)
        + rms_second * scaled_two
        - residual_mid
        * (rms_second * rms_second * rms_second)
        * jnp.mean(scaled_two * residual_mid, axis=1, keepdims=True)
    )
    gain_two = jnp.sum(grad_normed2 * residual_mid * rms_second, axis=0)
    mid_all = gather_rows(grad_mid.astype(jnp.bfloat16))
    grad_mixer_in = jnp.dot(mid_all, full_out, preferred_element_type=jnp.float32)
    grad_wout = jnp.einsum("rd,rc->dc", mid_all, mixer_in, preferred_element_type=jnp.float32)
    grad_conv_out = grad_mixer_in * proj_c
    grad_gated = (
        conv_weight[0] * grad_conv_out
        + conv_weight[1] * advanced(grad_conv_out * first_keep, 1)
        + conv_weight[2] * advanced(grad_conv_out * second_keep, 2)
    )
    grad_taps = jnp.stack(
        [
            jnp.sum(grad_conv_out * gated_in, axis=0),
            jnp.sum(grad_conv_out * first_keep * delayed(gated_in, 1), axis=0),
            jnp.sum(grad_conv_out * second_keep * delayed(gated_in, 2), axis=0),
        ]
    )
    grad_proj = jnp.concatenate(
        [grad_gated * proj_x, grad_mixer_in * conv_out, grad_gated * proj_b], axis=1
    ).astype(jnp.bfloat16)
    grad_win = jnp.einsum("rd,rf->df", first_all, grad_proj, preferred_element_type=jnp.float32)
    grad_mix = jnp.concatenate(
        [grad_win.astype(jnp.bfloat16), grad_wout.astype(jnp.bfloat16)], axis=1
    )
    sum_mix = scatter_blocks(grad_mix, "dp")
    grad_normed1 = scatter_rows(
        jnp.einsum("rf,df->rd", grad_proj, full_in, preferred_element_type=jnp.float32)
    )
    scaled_one = grad_normed1 * norm_gains[0]
    grad_tokens = (
        grad_mid
        + rms_first * scaled_one
        - x_float
        * (rms_first * rms_first * rms_first)
        * jnp.mean(scaled_one * x_float, axis=1, keepdims=True)
    ).astype(jnp.bfloat16)
    gain_one = jnp.sum(grad_normed1 * x_float * rms_first, axis=0)
    model_width = tokens.shape[1]
    sums = butterfly_sum(
        jnp.concatenate([gain_one, gain_two, grad_taps.reshape(-1)]).reshape(-1, 128), "dp"
    ).reshape(-1)
    gain_sums = butterfly_sum(sums[: 2 * model_width].reshape(2, model_width), "tensor")
    grad_conv = sums[2 * model_width :].reshape(grad_taps.shape)
    split = taken * chan_count
    shard_in = sum_mix[:, :split].astype(jnp.float32).reshape(w_in.shape)
    shard_out = sum_mix[:, split:].astype(jnp.float32).T
    shard_gu = sum_gu.astype(jnp.float32).reshape(w_gate_up.shape)
    shard_down = sum_down.astype(jnp.float32).T
    return (block_out, grad_tokens, shard_in, shard_out, shard_gu, shard_down, grad_conv, gain_sums)


MESH = pl.DeviceIdType.MESH
F32 = jnp.float32
BF16 = jnp.bfloat16
SPLIT = 2


def dot_nn(a, b):
    return jnp.dot(a, b, preferred_element_type=F32)


def dot_nt(a, b):
    return lax.dot_general(a, b, (((1,), (1,)), ((), ())), preferred_element_type=F32)


def dot_tn(a, b):
    return lax.dot_general(a, b, (((0,), (0,)), ((), ())), preferred_element_type=F32)


class Slots:
    def __init__(self):
        self.count = 0

    def take(self, number):
        first = self.count
        self.count += number
        return first


class Plan:
    def __init__(self, depth, rows, width, shard, chan, hidden):
        self.depth, self.rows, self.width, self.shard = depth, rows, width, shard
        self.cq, self.fq = chan // 2, hidden // 2
        self.cuts = 3 if self.fq % 384 == 0 else 1
        self.fc = self.fq // self.cuts
        self.part = rows // SPLIT
        cq, fc = self.cq, self.fc
        self.mix = 4 * cq
        self.cols = self.mix + 3 * self.fq
        self.gather_segs = [(0, self.mix)] + [
            (self.mix + 3 * fc * n, 3 * fc) for n in range(self.cuts)
        ]
        self.gu_segs = [(self.mix + 3 * fc * n, 2 * fc) for n in range(self.cuts)]
        self.dn_segs = [(self.mix + 3 * fc * n + 2 * fc, fc) for n in range(self.cuts)]
        self.mix_segs = [(0, self.mix)]
        self.sum_segs = self.gu_segs + self.dn_segs + self.mix_segs
        s = Slots()
        self.g_core = [s.take(1) for _ in self.gather_segs]
        self.g_z = [s.take(depth - 1) for _ in self.gather_segs]
        self.g_x = [s.take(depth) for _ in self.gather_segs]
        self.t_first, self.t_cot, self.t_second, self.t_mid = [s.take(3 * SPLIT) for _ in range(4)]
        self.u_out, self.u_gn2, self.u_blk, self.u_gn1 = [s.take(3 * SPLIT) for _ in range(4)]
        self.r_x = [s.take(depth) for _ in self.sum_segs]
        self.r_z = [s.take(depth - 1) for _ in self.sum_segs]
        self.r_c = [s.take(1) for _ in self.sum_segs]
        self.keep = s.take(1)
        self.small = s.take(3 + depth - 1)
        self.remote = s.count
        s = Slots()
        self.l_gather = [s.take(1) for _ in self.gather_segs]
        self.l_x, self.l_cot, self.l_keep, self.l_spill, self.l_stage = [s.take(1) for _ in range(5)]
        self.l_out = s.take(2)
        self.l_blk, self.l_tok = s.take(1), s.take(1)
        self.local = s.count


def block_kernel(
    plan, x_in, cot_in, keep_in, packed, taps_in, gains,
    blk_out, tok_out, grads_out, sums_out, xr, zr, spilled,
    w, nfm, ns, cot, proj, gg, ha, mix, rd_a, rd_b, ry_a, ry_b, sd, sy_a,
    own, mid_res, cr, keep, ostage, small_send, small_recv,
    ssem, rsem, lsem,
):
    p = plan
    depth, rows, part, shard, width = p.depth, p.rows, p.part, p.shard, p.width
    group = 2 * rows
    i = lax.axis_index("dp")
    y = lax.axis_index("tensor")
    core = lax.rem(i, 2)
    chip = i // 2
    x = lax.rem(chip, 2)
    z = chip // 2
    sib = (i + 1 - 2 * core, y)
    over = (i, 1 - y)
    aside = (i + 2 - 4 * x, y)

    def along(k):
        return (lax.rem(z + k, depth) * 4 + x * 2 + core, y)

    def sender(k):
        return lax.rem(z - k + depth, depth)

    def at(first, size):
        return pl.ds(pl.multiple_of(first, size), size)

    def remote(src, dst, slot, device):
        return pltpu.make_async_remote_copy(
            src_ref=src, dst_ref=dst, send_sem=ssem.at[slot], recv_sem=rsem.at[slot],
            device_id=device, device_id_type=MESH,
        )

    def local(src, dst, slot):
        return pltpu.make_async_copy(src, dst, lsem.at[slot])

    barrier = pltpu.get_barrier_semaphore()
    partners = [sib, over, aside] + [along(k) for k in range(1, depth)]
    for device in partners:
        pl.semaphore_signal(barrier, inc=1, device_id=device, device_id_type=MESH)
    x_copy = local(x_in, ry_b, p.l_x)
    x_copy.start()
    mine = at(i * shard, shard)
    gather_local = []
    for s, (lo, size) in enumerate(p.gather_segs):
        c = local(packed.at[core, :, lo : lo + size], w.at[mine, lo : lo + size], p.l_gather[s])
        c.start()
        gather_local.append(c)
    slot0 = (core * 2 + y) * rows
    cot_local = local(cot_in, cot.at[at(slot0, rows), :], p.l_cot)
    cot_local.start()
    keep_local = local(keep_in, keep.at[core], p.l_keep)
    keep_local.start()
    pl.semaphore_wait(barrier, len(partners))

    core_sends = [
        remote(packed.at[1 - core, :, lo : lo + size], w.at[mine, lo : lo + size], p.g_core[s], sib)
        for s, (lo, size) in enumerate(p.gather_segs)
    ]
    keep_send = remote(keep_in, keep.at[core], p.keep, sib)

    def chip_block(zz, xx):
        return at((zz * 2 + xx) * 2 * shard, 2 * shard)

    def gather_copies(s):
        lo, size = p.gather_segs[s]
        piece = w.at[chip_block(z, x), lo : lo + size]
        return [remote(piece, piece, p.g_z[s] + k - 1, along(k)) for k in range(1, depth)] + [
            remote(piece, piece, p.g_x[s], aside)
        ]

    def forward_copies(s):
        lo, size = p.gather_segs[s]
        out = []
        for k in range(1, depth):
            piece = w.at[chip_block(sender(k), x), lo : lo + size]
            out.append(remote(piece, piece, p.g_x[s] + k, aside))
        return out

    def gather_start(s):
        gather_local[s].wait()
        core_sends[s].wait_recv()
        for c in gather_copies(s):
            c.start()

    def gather_forward(s):
        arrived, onward = gather_copies(s), forward_copies(s)
        for k in range(depth - 1):
            arrived[k].wait_recv()
            onward[k].start()

    def gather_done(s):
        gather_copies(s)[depth - 1].wait_recv()
        for c in forward_copies(s):
            c.wait_recv()

    def gather_sent(s):
        for c in gather_copies(s) + forward_copies(s):
            c.wait_send()
        core_sends[s].wait_send()

    def rows_of(g, t, h):
        return at((g * 2 + t) * rows + h * part, part)

    def token_copy(buffer, base, kind, h):
        g, t = (core, y) if kind < 2 else (core, 1 - y)
        device = over if kind == 1 else sib
        piece = buffer.at[rows_of(g, t, h), :]
        return remote(piece, piece, base + kind * SPLIT + h, device)

    def tokens_send(buffer, base, h):
        token_copy(buffer, base, 1, h).start()
        token_copy(buffer, base, 0, h).start()

    def tokens_sent(buffer, base):
        for h in range(SPLIT):
            for kind in range(3):
                token_copy(buffer, base, kind, h).wait_send()

    def source(step):
        kind = step // SPLIT
        g = jnp.where(kind % 2 == 0, core, 1 - core)
        t = jnp.where(kind // 2 == 0, y, 1 - y)
        return kind, g, t, step % SPLIT

    def tokens_wait(buffer, base, step):
        kind, g, t, h = source(step)

        @pl.when(kind > 0)
        def _():
            piece = buffer.at[rows_of(g, t, h), :]
            remote(piece, piece, base + (kind - 1) * SPLIT + h, sib).wait_recv()

        @pl.when(kind == 2)
        def _():
            piece = buffer.at[rows_of(g, t, h), :]
            remote(piece, piece, base + 2 * SPLIT + h, sib).start()

        return rows_of(g, t, h)

    steps = 4 * SPLIT

    def core_copy(base, recv, q):
        piece = at(q * part, part)
        return remote(sd.at[piece, :], recv.at[piece, :], base + q, sib)

    def over_copy(base, send, recv, h):
        piece = at(h * part, part)
        return remote(send.at[piece, :], recv.at[piece, :], base + 2 * SPLIT + h, over)

    def partials(base, product, recv, send, recv_over, keep_own):
        def to_sibling(q, carry):
            t, h = jnp.where(q // SPLIT == 0, 1 - y, y), q % SPLIT
            n = t * SPLIT + h
            sd[at(n * part, part), :] = product(rows_of(1 - core, t, h)).astype(BF16)
            core_copy(base, recv, n).start()
            return carry

        lax.fori_loop(0, 2 * SPLIT, to_sibling, 0)

        def to_over(h, carry):
            n = (1 - y) * SPLIT + h
            value = product(rows_of(core, 1 - y, h))
            core_copy(base, recv, n).wait_recv()
            value = value + recv[at(n * part, part), :].astype(F32)
            send[at(h * part, part), :] = value.astype(BF16)
            over_copy(base, send, recv_over, h).start()
            return carry

        lax.fori_loop(0, SPLIT, to_over, 0)

        def to_own(h, carry):
            n = y * SPLIT + h
            value = product(rows_of(core, y, h))
            core_copy(base, recv, n).wait_recv()
            keep_own(at(h * part, part), value + recv[at(n * part, part), :].astype(F32))
            return carry

        lax.fori_loop(0, SPLIT, to_own, 0)
        for q in range(2 * SPLIT):
            core_copy(base, recv, q).wait_send()

    def x_copy_of(n, zz):
        lo, size = p.sum_segs[n]
        return remote(
            w.at[chip_block(zz, 1 - x), lo : lo + size], xr.at[zz, :, lo : lo + size],
            p.r_x[n] + zz, aside,
        )

    def z_copy_of(n, k):
        lo, size = p.sum_segs[n]
        zz = lax.rem(z + k, depth)
        return remote(
            w.at[chip_block(zz, x), lo : lo + size], zr.at[k - 1, :, lo : lo + size],
            p.r_z[n] + k - 1, along(k),
        )

    def c_copy_of(n):
        lo, size = p.sum_segs[n]
        theirs = at((i + 1 - 2 * core) * shard, shard)
        return remote(w.at[theirs, lo : lo + size], cr.at[:, lo : lo + size], p.r_c[n], sib)

    def reduce_x(n):
        lo, size = p.sum_segs[n]
        for k in list(range(1, depth)) + [0]:
            zz = lax.rem(z + k, depth)
            x_copy_of(n, zz).wait_recv()
            c = local(xr.at[zz, :, lo : lo + size], gg.at[0 : 2 * shard, 0:size], p.l_stage)
            c.start()
            c.wait()
            piece = chip_block(zz, x)
            w[piece, lo : lo + size] = (
                w[piece, lo : lo + size].astype(F32) + gg[0 : 2 * shard, 0:size].astype(F32)
            ).astype(BF16)
            if k:
                z_copy_of(n, k).start()

    def reduce_z(n, wait_before):
        lo, size = p.sum_segs[n]
        for k in range(1, depth):
            z_copy_of(n, k).wait_recv()
        first, last = 2 * shard, 2 * shard * depth
        for k in range(1, depth):
            c = local(
                zr.at[k - 1, :, lo : lo + size],
                gg.at[first + (k - 1) * 2 * shard : first + k * 2 * shard, 0:size],
                p.l_stage,
            )
            c.start()
            c.wait()
        mine_at, theirs_at = core * shard, (1 - core) * shard

        def total(offset):
            base = chip * 2 * shard + offset
            value = w[at(base, shard), lo : lo + size].astype(F32)
            for k in range(1, depth):
                value = value + gg[at(k * 2 * shard + offset, shard), 0:size].astype(F32)
            return value

        w[at((i + 1 - 2 * core) * shard, shard), lo : lo + size] = total(theirs_at).astype(BF16)
        c_copy_of(n).start()
        if wait_before:
            out_wait(0)
        ostage[0, :, 0:size] = total(mine_at)
        local(ostage.at[0, :, 0:size], grads_out.at[core, :, lo : lo + size], p.l_out).start()
        last_out[0] = size

    last_out = [0, 0]

    def out_wait(which):
        size = last_out[which]
        local(ostage.at[which, :, 0:size], grads_out.at[0, :, 0:size], p.l_out + which).wait()

    def reduce_core(n, wait_before):
        lo, size = p.sum_segs[n]
        c_copy_of(n).wait_recv()
        if wait_before:
            out_wait(1)
        ostage[1, :, 0:size] = cr[:, lo : lo + size].astype(F32)
        local(
            ostage.at[1, :, 0:size], grads_out.at[1 - core, :, lo : lo + size], p.l_out + 1
        ).start()
        last_out[1] = size

    for c in core_sends[:1]:
        c.start()
    gain0, gain1 = gains[0:1, :], gains[1:2, :]
    x_copy.wait()
    for h in range(SPLIT):
        xf = ry_b[h * part : (h + 1) * part, :].astype(F32)
        rms = lax.rsqrt(jnp.mean(xf * xf, axis=1, keepdims=True) + epsilon)
        nfm[rows_of(core, y, h), :] = (xf * rms * gain0).astype(BF16)
        mid_res[h * part : (h + 1) * part, :] = xf
        tokens_send(nfm, p.t_first, h)
    gather_start(0)
    for c in core_sends[1:]:
        c.start()
    keep_send.start()
    small_send[...] = jnp.zeros_like(small_send)
    gather_forward(0)
    for s in range(1, len(p.gather_segs)):
        gather_start(s)
    cot_local.wait()
    for h in range(SPLIT):
        tokens_send(cot, p.t_cot, h)
    gather_done(0)

    def in_projection(step, carry):
        r = tokens_wait(nfm, p.t_first, step)
        proj[r, :] = dot_nn(nfm[r, :], w[:, 0 : 3 * p.cq]).astype(BF16)
        return carry

    lax.fori_loop(0, steps, in_projection, 0)
    tokens_sent(nfm, p.t_first)
    spill = local(nfm, spilled, p.l_spill)
    spill.start()
    gather_forward(1)
    keep_local.wait()
    keep_send.wait_recv()
    lanes = p.cq // 128

    def conv_terms(g, j):
        r = at(g * group, group)
        col = pl.multiple_of(j * 128, 128)
        b = proj[r, pl.ds(col, 128)].astype(F32)
        c = proj[r, pl.ds(pl.multiple_of(col + p.cq, 128), 128)].astype(F32)
        xv = proj[r, pl.ds(pl.multiple_of(col + 2 * p.cq, 128), 128)].astype(F32)
        k1 = keep[g, :, 0:128].astype(F32)
        k2 = keep[g, :, 128:256].astype(F32)
        t = taps_in[:, pl.ds(pl.multiple_of(core * p.cq + j * 128, 128), 128)]
        gated = b * xv
        d1 = pltpu.roll(gated, 1, 0) * k1
        d2 = pltpu.roll(gated, 2, 0) * k2
        conv = t[0:1] * gated + t[1:2] * d1 + t[2:3] * d2
        return r, col, b, c, xv, k1, k2, t, gated, d1, d2, conv

    def conv_forward(step, carry):
        g = jnp.where(step // lanes == 0, 1 - core, core)
        r, col, b, c, xv, k1, k2, t, gated, d1, d2, conv = conv_terms(g, step % lanes)
        mix[r, pl.ds(col, 128)] = (c * conv).astype(BF16)
        return carry

    lax.fori_loop(0, 2 * lanes, conv_forward, 0)

    def add_mid(r, value):
        mid_res[r, :] += value

    partials(
        p.u_out,
        lambda r: dot_nt(mix[r, :], w[:, 3 * p.cq : p.mix]),
        rd_a, sy_a, ry_a, add_mid,
    )
    spill.wait()
    if p.cuts > 1:
        gather_forward(2)
    for h in range(SPLIT):
        piece = slice(h * part, (h + 1) * part)
        over_copy(p.u_out, sy_a, ry_a, h).wait_recv()
        value = mid_res[piece, :] + ry_a[piece, :].astype(F32)
        mid_res[piece, :] = value
        rms = lax.rsqrt(jnp.mean(value * value, axis=1, keepdims=True) + epsilon)
        ns[rows_of(core, y, h), :] = (value * rms * gain1).astype(BF16)
        tokens_send(ns, p.t_second, h)
    for step in range(2 * SPLIT, 3 * SPLIT):
        tokens_wait(cot, p.t_cot, step)
    for s in range(3, len(p.gather_segs)):
        gather_forward(s)
    for step in list(range(SPLIT, 2 * SPLIT)) + list(range(3 * SPLIT, 4 * SPLIT)):
        tokens_wait(cot, p.t_cot, step)

    fc = p.fc
    for n in range(p.cuts):
        gather_done(1 + n)
        lo = p.gather_segs[1 + n][0]

        def hidden(step, carry, n=n, lo=lo):
            if n == 0:
                r = tokens_wait(ns, p.t_second, step)
            else:
                _, g, t, h = source(step)
                r = rows_of(g, t, h)
            gate = dot_nn(ns[r, :], w[:, lo : lo + fc])
            up = dot_nn(ns[r, :], w[:, lo + fc : lo + 2 * fc])
            act = dot_nn(cot[r, :], w[:, lo + 2 * fc : lo + 3 * fc])
            sig = jax.nn.sigmoid(gate)
            silu = gate * sig
            ha[r, n * fc : (n + 1) * fc] = (silu * up).astype(BF16)
            gg[r, 2 * n * fc : (2 * n + 1) * fc] = (
                act * up * sig * (1.0 + gate * (1.0 - sig))
            ).astype(BF16)
            gg[r, (2 * n + 1) * fc : (2 * n + 2) * fc] = (act * silu).astype(BF16)
            return carry

        lax.fori_loop(0, steps, hidden, 0)
    tokens_sent(cot, p.t_cot)
    tokens_sent(ns, p.t_second)
    for s in range(len(p.gather_segs)):
        gather_sent(s)
    keep_send.wait_send()

    def gn2_product(r):
        value = None
        for n, (lo, size) in enumerate(p.gu_segs):
            term = dot_nt(gg[r, 2 * n * fc : (2 * n + 2) * fc], w[:, lo : lo + size])
            value = term if value is None else value + term
        return value

    def set_own(r, value):
        own[r, :] = value

    for h in range(SPLIT):
        over_copy(p.u_out, sy_a, ry_a, h).wait_send()
    partials(p.u_gn2, gn2_product, rd_a, sy_a, ry_a, set_own)

    def grad_gate_up(zz, carry):
        d = at(zz * 4 * shard, 4 * shard)
        for n, (lo, size) in enumerate(p.gu_segs):
            w[d, lo : lo + size] = dot_tn(
                ns[:, d], gg[:, 2 * n * fc : (2 * n + 2) * fc]
            ).astype(BF16)
            x_copy_of(n, zz).start()
        return carry

    lax.fori_loop(0, depth, grad_gate_up, 0)
    for h in range(SPLIT):
        piece = slice(h * part, (h + 1) * part)
        over_copy(p.u_gn2, sy_a, ry_a, h).wait_recv()
        gn2 = own[piece, :] + ry_a[piece, :].astype(F32)
        res = mid_res[piece, :]
        rms = lax.rsqrt(jnp.mean(res * res, axis=1, keepdims=True) + epsilon)
        small_send[0, 1:2, :] += jnp.sum(gn2 * (res * rms), axis=0, keepdims=True)
        q = gn2 * gain1
        value = (
            cot[rows_of(core, y, h), :].astype(F32)
            + rms * q
            - res * (rms * rms * rms) * jnp.mean(q * res, axis=1, keepdims=True)
        )
        own[piece, :] = value
        nfm[rows_of(core, y, h), :] = value.astype(BF16)
        tokens_send(nfm, p.t_mid, h)

    def blk_product(r):
        value = None
        for n, (lo, size) in enumerate(p.dn_segs):
            term = dot_nt(ha[r, n * fc : (n + 1) * fc], w[:, lo : lo + size])
            value = term if value is None else value + term
        return value

    for h in range(SPLIT):
        over_copy(p.u_gn2, sy_a, ry_a, h).wait_send()
    partials(p.u_blk, blk_product, rd_b, sy_a, ry_b, add_mid)
    restore = local(spilled, ns, p.l_spill)
    restore.start()
    dn0 = p.cuts

    def grad_down(zz, carry):
        d = at(zz * 4 * shard, 4 * shard)
        for n, (lo, size) in enumerate(p.dn_segs):
            w[d, lo : lo + size] = dot_tn(cot[:, d], ha[:, n * fc : (n + 1) * fc]).astype(BF16)
            x_copy_of(dn0 + n, zz).start()
        return carry

    lax.fori_loop(0, depth, grad_down, 0)
    for n in range(p.cuts):
        reduce_x(n)

    grow = group
    gcol = p.cq

    def grad_mixer(step, carry):
        r = tokens_wait(nfm, p.t_mid, step)
        _, g, t, h = source(step)
        value = dot_nn(nfm[r, :], w[:, 3 * p.cq : p.mix]).astype(BF16)
        rr = at(grow + t * rows + h * part, part)

        @pl.when(g == 0)
        def _():
            gg[rr, 0:gcol] = value

        @pl.when(g == 1)
        def _():
            gg[rr, gcol : 2 * gcol] = value

        return carry

    lax.fori_loop(0, steps, grad_mixer, 0)

    def conv_backward(step, carry):
        g = jnp.where(step // lanes == 0, 1 - core, core)
        j = step % lanes
        r, col, b, c, xv, k1, k2, t, gated, d1, d2, conv = conv_terms(g, j)
        gm = gg[grow : 2 * grow, pl.ds(pl.multiple_of(g * gcol + j * 128, 128), 128)].astype(F32)
        gco = gm * c
        grad_gated = (
            t[0:1] * gco
            + t[1:2] * pltpu.roll(gco * k1, group - 1, 0)
            + t[2:3] * pltpu.roll(gco * k2, group - 2, 0)
        )
        place = pl.ds(pl.multiple_of((y * 2 + core) * p.cq + j * 128, 128), 128)
        for n, term in enumerate((gated, d1, d2)):
            small_send[0, 8 + n : 9 + n, place] += jnp.sum(gco * term, axis=0, keepdims=True)
        proj[r, pl.ds(col, 128)] = (grad_gated * xv).astype(BF16)
        proj[r, pl.ds(pl.multiple_of(col + p.cq, 128), 128)] = (gm * conv).astype(BF16)
        proj[r, pl.ds(pl.multiple_of(col + 2 * p.cq, 128), 128)] = (grad_gated * b).astype(BF16)
        return carry

    lax.fori_loop(0, 2 * lanes, conv_backward, 0)
    for h in range(SPLIT):
        piece = slice(h * part, (h + 1) * part)
        over_copy(p.u_blk, sy_a, ry_b, h).wait_recv()
        ha[piece, 0:width] = (mid_res[piece, :] + ry_b[piece, :].astype(F32)).astype(BF16)
    blk_copy = local(ha.at[0:rows, 0:width], blk_out, p.l_blk)
    blk_copy.start()
    for h in range(SPLIT):
        over_copy(p.u_blk, sy_a, ry_b, h).wait_send()

    def set_mid(r, value):
        mid_res[r, :] = value

    partials(
        p.u_gn1,
        lambda r: dot_nt(proj[r, :], w[:, 0 : 3 * p.cq]),
        rd_a, sy_a, ry_a, set_mid,
    )
    x_back = local(x_in, ha.at[rows : 2 * rows, 0:width], p.l_x)
    x_back.start()
    restore.wait()
    mx0 = 2 * p.cuts

    def grad_mix(zz, carry):
        d = at(zz * 4 * shard, 4 * shard)
        w[d, 0 : 3 * p.cq] = dot_tn(ns[:, d], proj[...]).astype(BF16)
        w[d, 3 * p.cq : p.mix] = dot_tn(nfm[:, d], mix[...]).astype(BF16)
        x_copy_of(mx0, zz).start()
        return carry

    lax.fori_loop(0, depth, grad_mix, 0)
    for n in range(p.cuts):
        reduce_x(dn0 + n)
    x_back.wait()
    for h in range(SPLIT):
        piece = slice(h * part, (h + 1) * part)
        over_copy(p.u_gn1, sy_a, ry_a, h).wait_recv()
        gn1 = mid_res[piece, :] + ry_a[piece, :].astype(F32)
        xf = ha[rows + h * part : rows + (h + 1) * part, 0:width].astype(F32)
        rms = lax.rsqrt(jnp.mean(xf * xf, axis=1, keepdims=True) + epsilon)
        small_send[0, 0:1, :] += jnp.sum(gn1 * (xf * rms), axis=0, keepdims=True)
        q = gn1 * gain0
        ha[2 * rows + h * part : 2 * rows + (h + 1) * part, 0:width] = (
            own[piece, :]
            + rms * q
            - xf * (rms * rms * rms) * jnp.mean(q * xf, axis=1, keepdims=True)
        ).astype(BF16)
    tok_copy = local(ha.at[2 * rows : 3 * rows, 0:width], tok_out, p.l_tok)
    tok_copy.start()

    def small_copy(n, k=0):
        device = (sib, over, aside)[n] if n < 3 else along(k)
        return remote(
            small_send.at[min(n, 3)], small_recv.at[n + max(k - 1, 0)],
            p.small + n + max(k - 1, 0), device,
        )

    def small_step(n):
        small_copy(n).wait_recv()
        small_send[n + 1] = small_send[n] + small_recv[n]

    small_copy(0).start()
    reduce_x(mx0)
    small_step(0)
    small_copy(1).start()
    for n in range(p.cuts):
        reduce_z(n, n > 0)
    small_step(1)
    small_copy(2).start()
    for n in range(p.cuts):
        reduce_core(n, n > 0)
    for n in range(p.cuts):
        reduce_z(dn0 + n, True)
    small_step(2)
    for k in range(1, depth):
        small_copy(3, k).start()
    for n in range(p.cuts):
        reduce_core(dn0 + n, True)
    reduce_z(mx0, True)
    total = small_send[3]
    for k in range(1, depth):
        small_copy(3, k).wait_recv()
        total = total + small_recv[3 + k - 1]
    sums_out[...] = total
    reduce_core(mx0, True)
    out_wait(0)
    out_wait(1)
    blk_copy.wait()
    tok_copy.wait()
    tokens_sent(nfm, p.t_mid)
    for h in range(SPLIT):
        over_copy(p.u_gn1, sy_a, ry_a, h).wait_send()
    for n in range(len(p.sum_segs)):
        for zz in range(depth):
            x_copy_of(n, zz).wait_send()
        for k in range(1, depth):
            z_copy_of(n, k).wait_send()
        c_copy_of(n).wait_send()
    for n in range(3):
        small_copy(n).wait_send()
    for k in range(1, depth):
        small_copy(3, k).wait_send()


def fused_body(depth, tokens, cotangent, lengths, w_in, w_out, w_gate_up, w_down, conv_weight, norm_gains):
    rows, width = tokens.shape
    shard, taken, chan = w_in.shape
    hidden = w_gate_up.shape[2]
    plan = Plan(depth, rows, width, shard, chan, hidden)
    cq, fc, cuts = plan.cq, plan.fc, plan.cuts
    row_count = 2 * rows
    position = positions(lengths[0], row_count)
    keep = jnp.concatenate(
        [
            jnp.broadcast_to((position >= n).astype(BF16)[:, None], (row_count, 128))
            for n in (1, 2)
        ],
        axis=1,
    )
    piece_in = w_in.reshape(shard, taken, 2, cq).transpose(2, 0, 1, 3).reshape(2, shard, taken * cq)
    piece_out = w_out.reshape(2, cq, shard).transpose(0, 2, 1)
    piece_gu = w_gate_up.reshape(shard, 2, 2, cuts, fc).transpose(2, 0, 3, 1, 4)
    piece_dn = w_down.reshape(2, cuts, fc, shard).transpose(0, 3, 1, 2)[:, :, :, None]
    piece_ff = jnp.concatenate([piece_gu, piece_dn], axis=3).reshape(2, shard, 3 * cuts * fc)
    packed = jnp.concatenate([piece_in, piece_out, piece_ff], axis=2)
    total = 4 * rows
    any_spec = pl.BlockSpec(memory_space=pl.ANY)
    vmem_spec = pl.BlockSpec(memory_space=pltpu.VMEM)
    shape = jax.ShapeDtypeStruct
    outs = (
        shape((rows, width), BF16),
        shape((rows, width), BF16),
        shape((2, shard, plan.cols), F32),
        shape((16, width), F32),
        shape((depth, 2 * shard, plan.cols), BF16),
        shape((depth - 1, 2 * shard, plan.cols), BF16),
        shape((total, width), BF16),
    )
    vm = pltpu.VMEM
    block_out, grad_tokens, grads, sums, _, _, _ = pl.pallas_call(
        functools.partial(block_kernel, plan),
        out_shape=outs,
        in_specs=[any_spec, any_spec, any_spec, any_spec, vmem_spec, vmem_spec],
        out_specs=(any_spec, any_spec, any_spec, vmem_spec, any_spec, any_spec, any_spec),
        scratch_shapes=[
            vm((width, plan.cols), BF16),
            vm((total, width), BF16),
            vm((total, width), BF16),
            vm((total, width), BF16),
            vm((total, 3 * cq), BF16),
            vm((total, 2 * plan.fq), BF16),
            vm((total, plan.fq), BF16),
            vm((total, cq), BF16),
            vm((2 * rows, width), BF16),
            vm((2 * rows, width), BF16),
            vm((rows, width), BF16),
            vm((rows, width), BF16),
            vm((2 * rows, width), BF16),
            vm((rows, width), BF16),
            vm((rows, width), F32),
            vm((rows, width), F32),
            vm((shard, plan.cols), BF16),
            vm((2, row_count, 256), BF16),
            vm((2, shard, plan.mix if cuts > 1 else max(plan.mix, 2 * fc)), F32),
            vm((4, 16, width), F32),
            vm((3 + depth - 1, 16, width), F32),
            pltpu.SemaphoreType.DMA((plan.remote,)),
            pltpu.SemaphoreType.DMA((plan.remote,)),
            pltpu.SemaphoreType.DMA((plan.local,)),
        ],
        compiler_params=pltpu.CompilerParams(
            collective_id=0, has_side_effects=True, vmem_limit_bytes=63 * 2**20
        ),
    )(tokens, cotangent, keep, packed, conv_weight, norm_gains)
    ff = grads[:, :, plan.mix :].reshape(2, shard, cuts, 3, fc)
    grad_in = grads[:, :, : taken * cq].reshape(2, shard, taken, cq).transpose(1, 2, 0, 3)
    grad_out = grads[:, :, taken * cq : plan.mix].transpose(0, 2, 1)
    grad_gu = ff[:, :, :, :2].transpose(1, 3, 0, 2, 4)
    grad_dn = ff[:, :, :, 2].transpose(0, 2, 3, 1)
    y = lax.axis_index("tensor")
    grad_taps = lax.dynamic_slice(sums, (8, y * chan), (conv_weight.shape[0], chan))
    return (
        block_out,
        grad_tokens,
        grad_in.reshape(w_in.shape),
        grad_out.reshape(w_out.shape),
        grad_gu.reshape(w_gate_up.shape),
        grad_dn.reshape(w_down.shape),
        grad_taps,
        sums[:2],
    )


def solution(mesh):
    dp, tensor = mesh.shape["dp"], mesh.shape["tensor"]
    grouped = tensor == 2 and dp % 4 == 0 and dp >= 8
    return jax.shard_map(
        functools.partial(fused_body, dp // 4) if grouped else body,
        mesh=mesh,
        in_specs=(
            P(("dp", "tensor"), None),
            P(("dp", "tensor"), None),
            P("dp", None),
            P("dp", None, "tensor"),
            P("tensor", "dp"),
            P("dp", None, "tensor"),
            P("tensor", "dp"),
            P(None, "tensor"),
            P(),
        ),
        out_specs=(
            P(("dp", "tensor"), None),
            P(("dp", "tensor"), None),
            P("dp", None, "tensor"),
            P("tensor", "dp"),
            P("dp", None, "tensor"),
            P("tensor", "dp"),
            P(None, "tensor"),
            P(),
        ),
        check_vma=False,
    )
```

```python
import functools

import jax
import jax.numpy as jnp
from jax import lax
from jax.experimental import pallas as pl
from jax.experimental.pallas import tpu as pltpu
from jax.sharding import PartitionSpec as P

epsilon = 1e-05


def sequence_starts(seq_lengths):
    count = seq_lengths.shape[0]
    before = jnp.arange(count)[None, :] < jnp.arange(count)[:, None]
    return jnp.sum(jnp.where(before, seq_lengths[None, :], 0), axis=1)


def positions(seq_lengths, row_count):
    starts = sequence_starts(seq_lengths)
    row_index = jnp.arange(row_count, dtype=jnp.int32)
    begun_at = jnp.where(starts[None, :] <= row_index[:, None], starts[None, :], jnp.int32(0))
    return row_index - jnp.max(begun_at, axis=1)


def delayed(values, steps):
    return jnp.concatenate([jnp.zeros((steps, values.shape[1]), values.dtype), values[:-steps]], 0)


def advanced(values, steps):
    return jnp.concatenate([values[steps:], jnp.zeros((steps, values.shape[1]), values.dtype)], 0)


def gather_rows(values):
    count = lax.axis_size("tensor")
    if count != 2:
        return lax.all_gather(values, "tensor", axis=0, tiled=True)
    rows = values.shape[0]
    index = lax.axis_index("tensor")
    other = lax.ppermute(values, "tensor", [(0, 1), (1, 0)])
    whole = jnp.zeros((2 * rows, values.shape[1]), values.dtype)
    whole = lax.dynamic_update_slice_in_dim(whole, values, index * rows, 0)
    return lax.dynamic_update_slice_in_dim(whole, other, (1 - index) * rows, 0)


def scatter_rows(values):
    count = lax.axis_size("tensor")
    if count != 2:
        return lax.psum_scatter(
            values.astype(jnp.bfloat16), "tensor", scatter_dimension=0, tiled=True
        ).astype(jnp.float32)
    rows = values.shape[0] // 2
    index = lax.axis_index("tensor")
    away = lax.dynamic_slice_in_dim(values, (1 - index) * rows, rows, 0).astype(jnp.bfloat16)
    other = lax.ppermute(away, "tensor", [(0, 1), (1, 0)])
    return lax.dynamic_slice_in_dim(values, index * rows, rows, 0) + other.astype(jnp.float32)


def butterfly_sum(values, axis):
    count = lax.axis_size(axis)
    if count & (count - 1):
        return lax.psum(values, axis)
    step = 1
    while step < count:
        values = values + lax.ppermute(values, axis, [(i, i ^ step) for i in range(count)])
        step *= 2
    return values


def gather_blocks(shard, axis):
    count = lax.axis_size(axis)
    if count & (count - 1):
        return lax.all_gather(shard, axis, axis=0, tiled=True)
    index = lax.axis_index(axis)
    blocks = shard[None]
    step = count // 2
    while step >= 1:
        other = lax.ppermute(blocks, axis, [(i, i ^ step) for i in range(count)])
        upper = (index // step) % 2 == 1
        first = jnp.where(upper, other, blocks)
        second = jnp.where(upper, blocks, other)
        blocks = jnp.stack([first, second], axis=1).reshape((-1,) + shard.shape)
        step //= 2
    return blocks.reshape((-1,) + shard.shape[1:])


def scatter_blocks(values, axis):
    count = lax.axis_size(axis)
    if count & (count - 1):
        return lax.psum_scatter(values, axis, scatter_dimension=0, tiled=True)
    index = lax.axis_index(axis)
    shape = (values.shape[0] // count,) + values.shape[1:]
    step = 1
    while step < count:
        pairs = values.reshape((count // step // 2, 2) + shape)
        side = (index // step) % 2
        away = lax.dynamic_index_in_dim(pairs, 1 - side, 1, keepdims=False)
        kept = lax.dynamic_index_in_dim(pairs, side, 1, keepdims=False)
        other = lax.ppermute(away, axis, [(i, i ^ step) for i in range(count)])
        values = (kept.astype(jnp.float32) + other.astype(jnp.float32)).astype(values.dtype)
        step *= 2
    return values.reshape(shape)


def body(tokens, cotangent, lengths, w_in, w_out, w_gate_up, w_down, conv_weight, norm_gains):
    shard_rows, taken, chan_count = w_in.shape
    hidden = w_gate_up.shape[2]
    packed = jnp.concatenate([w_in.reshape(shard_rows, taken * chan_count), w_out.T], axis=1)
    full_mix = lax.all_gather(packed, "dp", axis=0, tiled=True)
    full_gu = lax.all_gather(
        w_gate_up.reshape(shard_rows, 2 * hidden), "dp", axis=0, tiled=True
    )
    full_down = gather_blocks(w_down.T, "dp")
    full_in = full_mix[:, : taken * chan_count]
    full_out = full_mix[:, taken * chan_count :]
    x_float = tokens.astype(jnp.float32)
    rms_first = lax.rsqrt(jnp.mean(x_float * x_float, axis=1, keepdims=True) + epsilon)
    normed_first = (x_float * rms_first * norm_gains[0]).astype(jnp.bfloat16)
    first_all = gather_rows(normed_first)
    cot_all = gather_rows(cotangent)
    row_count = first_all.shape[0]
    position = positions(lengths[0], row_count)
    first_keep = (position >= 1).astype(jnp.float32)[:, None]
    second_keep = (position >= 2).astype(jnp.float32)[:, None]
    projected = jnp.dot(first_all, full_in, preferred_element_type=jnp.float32)
    proj_b = projected[:, :chan_count]
    proj_c = projected[:, chan_count : 2 * chan_count]
    proj_x = projected[:, 2 * chan_count :]
    gated_in = proj_b * proj_x
    conv_out = (
        conv_weight[0] * gated_in
        + conv_weight[1] * delayed(gated_in, 1) * first_keep
        + conv_weight[2] * delayed(gated_in, 2) * second_keep
    )
    mixer_in = (proj_c * conv_out).astype(jnp.bfloat16)
    residual_mid = x_float + scatter_rows(
        jnp.einsum("rc,dc->rd", mixer_in, full_out, preferred_element_type=jnp.float32)
    )
    rms_second = lax.rsqrt(jnp.mean(residual_mid * residual_mid, axis=1, keepdims=True) + epsilon)
    normed_second = (residual_mid * rms_second * norm_gains[1]).astype(jnp.bfloat16)
    second_all = gather_rows(normed_second)
    gate_up = jnp.dot(second_all, full_gu, preferred_element_type=jnp.float32)
    gate_pre = gate_up[:, :hidden]
    up_pre = gate_up[:, hidden:]
    sig_gate = jax.nn.sigmoid(gate_pre)
    hidden_act = (gate_pre * sig_gate * up_pre).astype(jnp.bfloat16)
    grad_down = jnp.einsum("rd,rf->df", cot_all, hidden_act, preferred_element_type=jnp.float32)
    grad_down, full_down = lax.optimization_barrier((grad_down.astype(jnp.bfloat16), full_down))
    sum_down = lax.psum_scatter(grad_down, "dp", scatter_dimension=0, tiled=True)
    grad_act = jnp.einsum("rd,df->rf", cot_all, full_down, preferred_element_type=jnp.float32)
    grad_gate = (grad_act * up_pre * sig_gate * (1.0 + gate_pre * (1.0 - sig_gate))).astype(
        jnp.bfloat16
    )
    grad_up = (grad_act * gate_pre * sig_gate).astype(jnp.bfloat16)
    grad_hidden = jnp.concatenate([grad_gate, grad_up], axis=1)
    grad_gu = jnp.einsum("rd,rf->df", second_all, grad_hidden, preferred_element_type=jnp.float32)
    grad_gu, grad_gate, grad_up = lax.optimization_barrier(
        (grad_gu.astype(jnp.bfloat16), grad_gate, grad_up)
    )
    grad_hidden = jnp.concatenate([grad_gate, grad_up], axis=1)
    grad_gu, sum_down = lax.optimization_barrier((grad_gu, sum_down))
    sum_gu = lax.psum_scatter(grad_gu, "dp", scatter_dimension=0, tiled=True)
    grad_normed2 = scatter_rows(
        jnp.einsum("rf,df->rd", grad_hidden, full_gu, preferred_element_type=jnp.float32)
    )
    block_out = (
        residual_mid
        + scatter_rows(
            jnp.einsum("rf,df->rd", hidden_act, full_down, preferred_element_type=jnp.float32)
        )
    ).astype(jnp.bfloat16)
    scaled_two = grad_normed2 * norm_gains[1]
    grad_mid = (
        cotangent.astype(jnp.float32)
        + rms_second * scaled_two
        - residual_mid
        * (rms_second * rms_second * rms_second)
        * jnp.mean(scaled_two * residual_mid, axis=1, keepdims=True)
    )
    gain_two = jnp.sum(grad_normed2 * residual_mid * rms_second, axis=0)
    mid_all = gather_rows(grad_mid.astype(jnp.bfloat16))
    grad_mixer_in = jnp.dot(mid_all, full_out, preferred_element_type=jnp.float32)
    grad_wout = jnp.einsum("rd,rc->dc", mid_all, mixer_in, preferred_element_type=jnp.float32)
    grad_conv_out = grad_mixer_in * proj_c
    grad_gated = (
        conv_weight[0] * grad_conv_out
        + conv_weight[1] * advanced(grad_conv_out * first_keep, 1)
        + conv_weight[2] * advanced(grad_conv_out * second_keep, 2)
    )
    grad_taps = jnp.stack(
        [
            jnp.sum(grad_conv_out * gated_in, axis=0),
            jnp.sum(grad_conv_out * first_keep * delayed(gated_in, 1), axis=0),
            jnp.sum(grad_conv_out * second_keep * delayed(gated_in, 2), axis=0),
        ]
    )
    grad_proj = jnp.concatenate(
        [grad_gated * proj_x, grad_mixer_in * conv_out, grad_gated * proj_b], axis=1
    ).astype(jnp.bfloat16)
    grad_win = jnp.einsum("rd,rf->df", first_all, grad_proj, preferred_element_type=jnp.float32)
    grad_mix = jnp.concatenate(
        [grad_win.astype(jnp.bfloat16), grad_wout.astype(jnp.bfloat16)], axis=1
    )
    sum_mix = scatter_blocks(grad_mix, "dp")
    grad_normed1 = scatter_rows(
        jnp.einsum("rf,df->rd", grad_proj, full_in, preferred_element_type=jnp.float32)
    )
    scaled_one = grad_normed1 * norm_gains[0]
    grad_tokens = (
        grad_mid
        + rms_first * scaled_one
        - x_float
        * (rms_first * rms_first * rms_first)
        * jnp.mean(scaled_one * x_float, axis=1, keepdims=True)
    ).astype(jnp.bfloat16)
    gain_one = jnp.sum(grad_normed1 * x_float * rms_first, axis=0)
    model_width = tokens.shape[1]
    sums = butterfly_sum(
        jnp.concatenate([gain_one, gain_two, grad_taps.reshape(-1)]).reshape(-1, 128), "dp"
    ).reshape(-1)
    gain_sums = butterfly_sum(sums[: 2 * model_width].reshape(2, model_width), "tensor")
    grad_conv = sums[2 * model_width :].reshape(grad_taps.shape)
    split = taken * chan_count
    shard_in = sum_mix[:, :split].astype(jnp.float32).reshape(w_in.shape)
    shard_out = sum_mix[:, split:].astype(jnp.float32).T
    shard_gu = sum_gu.astype(jnp.float32).reshape(w_gate_up.shape)
    shard_down = sum_down.astype(jnp.float32).T
    return (block_out, grad_tokens, shard_in, shard_out, shard_gu, shard_down, grad_conv, gain_sums)


MESH = pl.DeviceIdType.MESH
F32 = jnp.float32
BF16 = jnp.bfloat16
SPLIT = 2


def dot_nn(a, b):
    return jnp.dot(a, b, preferred_element_type=F32)


def dot_nt(a, b):
    return lax.dot_general(a, b, (((1,), (1,)), ((), ())), preferred_element_type=F32)


def dot_tn(a, b):
    return lax.dot_general(a, b, (((0,), (0,)), ((), ())), preferred_element_type=F32)


class Slots:
    def __init__(self):
        self.count = 0

    def take(self, number):
        first = self.count
        self.count += number
        return first


class Plan:
    def __init__(self, depth, rows, width, shard, chan, hidden):
        self.depth, self.rows, self.width, self.shard = depth, rows, width, shard
        self.cq, self.fq = chan // 2, hidden // 2
        self.cuts = 3 if self.fq % 384 == 0 else 1
        self.fc = self.fq // self.cuts
        self.part = rows // SPLIT
        cq, fc = self.cq, self.fc
        self.mix = 4 * cq
        self.cols = self.mix + 3 * self.fq
        self.gather_segs = [(0, 3 * cq), (3 * cq, cq)] + [
            (self.mix + 3 * fc * n, 3 * fc) for n in range(self.cuts)
        ]
        self.gu_segs = [(self.mix + 3 * fc * n, 2 * fc) for n in range(self.cuts)]
        self.dn_segs = [(self.mix + 3 * fc * n + 2 * fc, fc) for n in range(self.cuts)]
        self.mix_segs = [(0, self.mix)]
        self.sum_segs = self.gu_segs + self.dn_segs + self.mix_segs
        self.kind_early = [0, self.cuts]
        self.kind_gu = list(range(1, self.cuts))
        self.kind_dn = list(range(self.cuts + 1, 2 * self.cuts))
        self.kind_mix = [2 * self.cuts]
        s = Slots()
        self.pieces = [
            [("in", k, 0, k * cq, cq) for k in range(3)],
            [("out", 0, 0, 3 * cq, cq)],
        ] + [
            [("gu", k, n * fc, self.mix + (3 * n + k) * fc, fc) for k in range(2)]
            + [("dn", 0, n * fc, self.mix + (3 * n + 2) * fc, fc)]
            for n in range(self.cuts)
        ]
        self.g_core = [s.take(len(pieces)) for pieces in self.pieces]
        self.g_z = [s.take(depth - 1) for _ in self.gather_segs]
        self.g_x = [s.take(depth) for _ in self.gather_segs]
        self.g_on = [s.take(depth - 1) for _ in self.gather_segs]
        self.t_first, self.t_cot, self.t_second, self.t_mid = [s.take(3 * SPLIT) for _ in range(4)]
        self.u_out, self.u_gn2, self.u_blk, self.u_gn1 = [s.take(3 * SPLIT) for _ in range(4)]
        self.r_x = [s.take(depth) for _ in self.sum_segs]
        self.r_z = [s.take(depth - 1) for _ in self.sum_segs]
        self.r_c = [s.take(1) for _ in self.sum_segs]
        self.keep = s.take(1)
        self.small = s.take(3 + depth - 1)
        self.remote = s.count
        s = Slots()
        self.l_gather = [s.take(len(pieces)) for pieces in self.pieces]
        self.l_x, self.l_cot, self.l_spill, self.l_proj = [s.take(1) for _ in range(4)]
        self.l_xr, self.l_zr = s.take(self.cuts), s.take(self.cuts * (depth - 1))
        self.l_out = [s.take(2 * 4) for _ in self.sum_segs]
        self.l_blk, self.l_tok = s.take(1), s.take(1)
        self.local = s.count


def block_kernel(
    plan, x_in, cot_in, lengths, in_in, out_in, gu_in, dn_in, taps_in, gains,
    blk_out, tok_out, in_out, out_out, gu_out, dn_out, sums_out, xr, zr, spilled, proj_held,
    w, nfm, ns, cot, proj, gg, ha, mix, rd_a, rd_b, ry_a, ry_b, sd, sy_a,
    own, mid_res, cr, keep, small_send, small_recv,
    ssem, rsem, lsem,
):
    p = plan
    depth, rows, part, shard, width = p.depth, p.rows, p.part, p.shard, p.width
    group = 2 * rows
    i = lax.axis_index("dp")
    y = lax.axis_index("tensor")
    core = lax.rem(i, 2)
    chip = i // 2
    x = lax.rem(chip, 2)
    z = chip // 2
    sib = (i + 1 - 2 * core, y)
    over = (i, 1 - y)
    aside = (i + 2 - 4 * x, y)

    def along(k):
        return (lax.rem(z + k, depth) * 4 + x * 2 + core, y)

    def sender(k):
        return lax.rem(z - k + depth, depth)

    def at(first, size):
        return pl.ds(pl.multiple_of(first, size), size)

    def remote(src, dst, slot, device):
        return pltpu.make_async_remote_copy(
            src_ref=src, dst_ref=dst, send_sem=ssem.at[slot], recv_sem=rsem.at[slot],
            device_id=device, device_id_type=MESH,
        )

    def local(src, dst, slot):
        return pltpu.make_async_copy(src, dst, lsem.at[slot])

    barrier = pltpu.get_barrier_semaphore()
    partners = [sib, over, aside] + [along(k) for k in range(1, depth)]
    for device in partners:
        pl.semaphore_signal(barrier, inc=1, device_id=device, device_id_type=MESH)
    x_copy = local(x_in, ry_b, p.l_x)
    x_copy.start()
    mine = at(i * shard, shard)

    def shard_piece(piece, for_core):
        name, index, first, lo, size = piece
        share = p.cq if name in ("in", "out") else p.fq
        col = pl.ds(pl.multiple_of(for_core * share + first, 128), size)
        if name == "in":
            return in_in.at[index, :, col], w.at[mine, lo : lo + size]
        if name == "gu":
            return gu_in.at[index, :, col], w.at[mine, lo : lo + size]
        return (out_in if name == "out" else dn_in).at[:, col], w.at[mine, lo : lo + size]

    gather_local = [
        [local(*shard_piece(piece, core), p.l_gather[s] + n) for n, piece in enumerate(pieces)]
        for s, pieces in enumerate(p.pieces)
    ]
    for copies in gather_local:
        for c in copies:
            c.start()
    slot0 = (core * 2 + y) * rows
    cot_local = local(cot_in, cot.at[at(slot0, rows), :], p.l_cot)
    cot_local.start()
    pl.semaphore_wait(barrier, len(partners))

    core_sends = [
        [
            remote(*shard_piece(piece, 1 - core), p.g_core[s] + n, sib)
            for n, piece in enumerate(pieces)
        ]
        for s, pieces in enumerate(p.pieces)
    ]
    keep_send = remote(keep.at[core], keep.at[core], p.keep, sib)

    def chip_block(zz, xx):
        return at((zz * 2 + xx) * 2 * shard, 2 * shard)

    def own_block(s):
        lo, size = p.gather_segs[s]
        return w.at[chip_block(z, x), lo : lo + size]

    def gather_z(s, k):
        return remote(own_block(s), own_block(s), p.g_z[s] + k - 1, along(k))

    def gather_x(s, k):
        lo, size = p.gather_segs[s]
        piece = w.at[chip_block(sender(k), x), lo : lo + size]
        return remote(piece, piece, p.g_x[s] + k, aside)

    line = depth == 4

    def direct(k):
        return {1: z != 3, 2: (z == 0) | (z == 3), 3: z != 0}[k] if line else k > 0

    def onward(k):
        return {1: z == 2, 2: (z == 1) | (z == 2), 3: z == 1}[k]

    def gather_on(s, k):
        lo, size = p.gather_segs[s]
        piece = w.at[chip_block(sender(k), x), lo : lo + size]
        end = jnp.where(z == 1, 0, 3)
        arrives = p.g_z[s] + lax.rem(end - z + k + depth, depth) - 1
        return pltpu.make_async_remote_copy(
            src_ref=piece, dst_ref=piece, send_sem=ssem.at[p.g_on[s] + k - 1],
            recv_sem=rsem.at[arrives], device_id=(end * 4 + x * 2 + core, y), device_id_type=MESH,
        )

    def gather_start(s):
        for c in gather_local[s]:
            c.wait()
        for c in core_sends[s]:
            c.wait_recv()
        for k in range(1, depth):

            @pl.when(direct(k))
            def _(k=k):
                gather_z(s, k).start()

        gather_x(s, 0).start()

    def gather_forward(s):
        for k in [3, 1, 2] if line else range(1, depth):
            gather_z(s, k).wait_recv()
            if line:

                @pl.when(onward(k))
                def _(k=k):
                    gather_on(s, k).start()

            gather_x(s, k).start()

    def gather_done(s):
        for k in range(depth):
            gather_x(s, k).wait_recv()

    def gather_sent(s):
        for k in range(1, depth):

            @pl.when(direct(k))
            def _(k=k):
                gather_z(s, k).wait_send()

            if line:

                @pl.when(onward(k))
                def _(k=k):
                    gather_on(s, k).wait_send()

        for k in range(depth):
            gather_x(s, k).wait_send()
        for c in core_sends[s]:
            c.wait_send()

    def rows_of(g, t, h):
        return at((g * 2 + t) * rows + h * part, part)

    def token_copy(buffer, base, kind, h):
        g, t = (core, y) if kind < 2 else (core, 1 - y)
        device = over if kind == 1 else sib
        piece = buffer.at[rows_of(g, t, h), :]
        return remote(piece, piece, base + kind * SPLIT + h, device)

    def tokens_send(buffer, base, h):
        token_copy(buffer, base, 1, h).start()
        token_copy(buffer, base, 0, h).start()

    def tokens_sent(buffer, base):
        for h in range(SPLIT):
            for kind in range(3):
                token_copy(buffer, base, kind, h).wait_send()

    def source(step):
        kind = step // SPLIT
        g = jnp.where(kind % 2 == 0, core, 1 - core)
        t = jnp.where(kind // 2 == 0, y, 1 - y)
        return kind, g, t, step % SPLIT

    def tokens_wait(buffer, base, step):
        kind, g, t, h = source(step)

        @pl.when(kind > 0)
        def _():
            piece = buffer.at[rows_of(g, t, h), :]
            remote(piece, piece, base + (kind - 1) * SPLIT + h, sib).wait_recv()

        @pl.when(kind == 2)
        def _():
            piece = buffer.at[rows_of(g, t, h), :]
            remote(piece, piece, base + 2 * SPLIT + h, sib).start()

        return rows_of(g, t, h)

    steps = 4 * SPLIT

    def core_copy(base, recv, q):
        piece = at(q * part, part)
        return remote(sd.at[piece, :], recv.at[piece, :], base + q, sib)

    def over_copy(base, send, recv, h):
        piece = at(h * part, part)
        return remote(send.at[piece, :], recv.at[piece, :], base + 2 * SPLIT + h, over)

    def partials(base, product, recv, send, recv_over, keep_own, hold=False, between=None, observe=None):
        def to_sibling(q, carry):
            t, h = jnp.where(q // SPLIT == 0, 1 - y, y), q % SPLIT
            n = t * SPLIT + h
            value = product(rows_of(1 - core, t, h))
            if observe:
                observe(rows_of(1 - core, t, h), value)
            sd[at(n * part, part), :] = value.astype(BF16)
            core_copy(base, recv, n).start()
            return carry

        lax.fori_loop(0, 2 * SPLIT, to_sibling, 0)

        def to_over(h, carry):
            n = (1 - y) * SPLIT + h
            value = product(rows_of(core, 1 - y, h))
            if observe:
                observe(rows_of(core, 1 - y, h), value)
            core_copy(base, recv, n).wait_recv()
            value = value + recv[at(n * part, part), :].astype(F32)
            send[at(h * part, part), :] = value.astype(BF16)
            if not hold:
                over_copy(base, send, recv_over, h).start()
            return carry

        lax.fori_loop(0, SPLIT, to_over, 0)
        if between:
            between()

        def to_own(h, carry):
            n = y * SPLIT + h
            value = product(rows_of(core, y, h))
            if observe:
                observe(rows_of(core, y, h), value)
            core_copy(base, recv, n).wait_recv()
            keep_own(at(h * part, part), value + recv[at(n * part, part), :].astype(F32))
            return carry

        lax.fori_loop(0, SPLIT, to_own, 0)
        for q in range(2 * SPLIT):
            core_copy(base, recv, q).wait_send()

    def grad_piece(n, first, size, early=True):
        lo, cols = p.sum_segs[n]
        if early and n in p.kind_early:
            base = 0 if n < p.cuts else width
            return proj.at[at(base + first, size), 0:cols]
        if n in p.kind_mix:
            return ha.at[at(group + first, size), 0:cols]
        return w.at[at(first, size), lo : lo + cols]

    def x_copy_of(n, k):
        lo, size = p.sum_segs[n]
        zz = lax.rem(z + k, depth)
        piece = grad_piece(n, (zz * 2 + 1 - x) * 2 * shard, 2 * shard)
        return remote(piece, xr.at[k, :, lo : lo + size], p.r_x[n] + k, aside)

    def z_copy_of(n, k):
        lo, size = p.sum_segs[n]
        zz = lax.rem(z + k, depth)
        piece = grad_piece(n, (zz * 2 + x) * 2 * shard, 2 * shard)
        return remote(piece, zr.at[k - 1, :, lo : lo + size], p.r_z[n] + k - 1, along(k))

    def c_copy_of(n):
        lo, size = p.sum_segs[n]
        piece = grad_piece(n, (i + 1 - 2 * core) * shard, shard, False)
        return remote(piece, cr.at[:, lo : lo + size], p.r_c[n], sib)

    def stage_place(kind, which, n, rank):
        number = kind.index(n)
        if kind is p.kind_early and which == "x":
            return sd, number * 2 * shard, 0
        return gg, rank * 2 * shard, sum(p.sum_segs[m][1] for m in kind[:number])

    def staged(kind, which, n, k):
        lo, size = p.sum_segs[n]
        number = kind.index(n)
        buffer, row, col = stage_place(kind, which, n, 0 if which == "x" else k)
        dst = buffer.at[row : row + 2 * shard, col : col + size]
        if which == "x":
            return local(xr.at[k, :, lo : lo + size], dst, p.l_xr + number)
        slot = p.l_zr + number * (depth - 1) + k - 1
        return local(zr.at[k - 1, :, lo : lo + size], dst, slot)

    def reduce_x(kind, k):
        zz = lax.rem(z + k, depth)
        for n in kind:
            x_copy_of(n, k).wait_recv()
            staged(kind, "x", n, k).start()
        for n in kind:
            size = p.sum_segs[n][1]
            buffer, row, col = stage_place(kind, "x", n, 0)
            staged(kind, "x", n, k).wait()
            piece = grad_piece(n, (zz * 2 + x) * 2 * shard, 2 * shard)
            piece[...] = (
                piece[...].astype(F32)
                + buffer[row : row + 2 * shard, col : col + size].astype(F32)
            ).astype(BF16)
            if k:
                z_copy_of(n, k).start()

    def out_copies(n, which):
        buffer, place = ((own, core), (mid_res, 1 - core))[which]
        held = slice(n * shard, (n + 1) * shard)
        if n < p.cuts:
            col = pl.ds(pl.multiple_of(place * p.fq + n * p.fc, 128), p.fc)
            parts = [(k * p.fc, p.fc, gu_out.at[k, :, col]) for k in range(2)]
        elif n < 2 * p.cuts:
            col = pl.ds(pl.multiple_of(place * p.fq + (n - p.cuts) * p.fc, 128), p.fc)
            parts = [(0, p.fc, dn_out.at[:, col])]
        else:
            col = pl.ds(pl.multiple_of(place * p.cq, 128), p.cq)
            parts = [(k * p.cq, p.cq, in_out.at[k, :, col]) for k in range(3)]
            parts.append((3 * p.cq, p.cq, out_out.at[:, col]))
        return [
            local(buffer.at[held, lo : lo + size], dst, p.l_out[n] + which * 4 + number)
            for number, (lo, size, dst) in enumerate(parts)
        ]

    def reduce_z(kind):
        for n in kind:
            for k in range(1, depth):
                z_copy_of(n, k).wait_recv()
                staged(kind, "z", n, k).start()
        for n in kind:
            size = p.sum_segs[n][1]
            for k in range(1, depth):
                staged(kind, "z", n, k).wait()

            def total(offset, n=n, size=size):
                value = grad_piece(n, chip * 2 * shard + offset, shard, False)[...].astype(F32)
                for k in range(1, depth):
                    _, row, col = stage_place(kind, "z", n, k)
                    value = value + gg[at(row + offset, shard), col : col + size].astype(F32)
                return value

            theirs = grad_piece(n, (i + 1 - 2 * core) * shard, shard, False)
            theirs[...] = total((1 - core) * shard).astype(BF16)
            c_copy_of(n).start()
            own[n * shard : (n + 1) * shard, 0:size] = total(core * shard)
            for c in out_copies(n, 0):
                c.start()

    def reduce_core(kind):
        for n in kind:
            lo, size = p.sum_segs[n]
            c_copy_of(n).wait_recv()
            mid_res[n * shard : (n + 1) * shard, 0:size] = cr[:, lo : lo + size].astype(F32)
            for c in out_copies(n, 1):
                c.start()

    def small_copy(n, k=0):
        device = (sib, over, aside)[n] if n < 3 else along(k)
        return remote(
            small_send.at[min(n, 3)], small_recv.at[n + max(k - 1, 0)],
            p.small + n + max(k - 1, 0), device,
        )

    def small_step(n):
        small_copy(n).wait_recv()
        small_send[n + 1] = small_send[n] + small_recv[n]

    for copies in core_sends[:2]:
        for c in copies:
            c.start()
    gain0, gain1 = gains[0:1, :], gains[1:2, :]
    x_copy.wait()
    for h in range(SPLIT):
        xf = ry_b[h * part : (h + 1) * part, :].astype(F32)
        rms = lax.rsqrt(jnp.mean(xf * xf, axis=1, keepdims=True) + epsilon)
        nfm[rows_of(core, y, h), :] = (xf * rms * gain0).astype(BF16)
        mid_res[h * part : (h + 1) * part, :] = xf
        tokens_send(nfm, p.t_first, h)
    gather_start(0)
    gather_start(1)
    for copies in core_sends[2:]:
        for c in copies:
            c.start()
    row = lax.broadcasted_iota(jnp.int32, (group, 128), 0)
    begun, start = jnp.zeros_like(row), 0
    for s in range(lengths.shape[1]):
        begun = jnp.where(row >= start, start, begun)
        start = start + lengths[0, s]
    for n in range(2):
        keep[core, :, 128 * n : 128 * (n + 1)] = jnp.where(
            row - begun >= n + 1, 1.0, 0.0
        ).astype(BF16)
    keep_send.start()
    small_send[...] = jnp.zeros_like(small_send)
    cot_local.wait()
    gather_forward(0)
    for h in range(SPLIT):
        tokens_send(cot, p.t_cot, h)
    gather_start(2)
    gather_forward(1)
    gather_done(0)

    def in_projection(step, carry):
        r = tokens_wait(nfm, p.t_first, step)
        proj[r, :] = dot_nn(nfm[r, :], w[:, 0 : 3 * p.cq]).astype(BF16)
        return carry

    lax.fori_loop(0, steps, in_projection, 0)
    tokens_sent(nfm, p.t_first)
    spill = local(nfm, spilled, p.l_spill)
    spill.start()
    hold = local(proj, proj_held, p.l_proj)
    hold.start()
    keep_send.wait_recv()
    gather_done(1)
    lanes = p.cq // 128

    def conv_terms(g, j):
        r = at(g * group, group)
        col = pl.multiple_of(j * 128, 128)
        b = proj[r, pl.ds(col, 128)].astype(F32)
        c = proj[r, pl.ds(pl.multiple_of(col + p.cq, 128), 128)].astype(F32)
        xv = proj[r, pl.ds(pl.multiple_of(col + 2 * p.cq, 128), 128)].astype(F32)
        k1 = keep[g, :, 0:128].astype(F32)
        k2 = keep[g, :, 128:256].astype(F32)
        t = taps_in[:, pl.ds(pl.multiple_of(core * p.cq + j * 128, 128), 128)]
        gated = b * xv
        d1 = pltpu.roll(gated, 1, 0) * k1
        d2 = pltpu.roll(gated, 2, 0) * k2
        conv = t[0:1] * gated + t[1:2] * d1 + t[2:3] * d2
        return r, col, b, c, xv, k1, k2, t, gated, d1, d2, conv

    def conv_forward(step, carry):
        g = jnp.where(step // lanes == 0, 1 - core, core)
        r, col, b, c, xv, k1, k2, t, gated, d1, d2, conv = conv_terms(g, step % lanes)
        mix[r, pl.ds(col, 128)] = (c * conv).astype(BF16)
        return carry

    lax.fori_loop(0, 2 * lanes, conv_forward, 0)

    def add_mid(r, value):
        mid_res[r, :] += value

    partials(
        p.u_out,
        lambda r: dot_nt(mix[r, :], w[:, 3 * p.cq : p.mix]),
        rd_a, sy_a, ry_a, add_mid,
    )
    spill.wait()
    for step in range(2 * SPLIT, 3 * SPLIT):
        tokens_wait(cot, p.t_cot, step)
    gather_forward(2)
    for s in range(3, min(4, len(p.gather_segs))):
        gather_start(s)
    for h in range(SPLIT):
        piece = slice(h * part, (h + 1) * part)
        over_copy(p.u_out, sy_a, ry_a, h).wait_recv()
        value = mid_res[piece, :] + ry_a[piece, :].astype(F32)
        mid_res[piece, :] = value
        rms = lax.rsqrt(jnp.mean(value * value, axis=1, keepdims=True) + epsilon)
        ns[rows_of(core, y, h), :] = (value * rms * gain1).astype(BF16)
        tokens_send(ns, p.t_second, h)
    for s in range(3, len(p.gather_segs)):
        if s == 3:
            gather_forward(s)
        else:
            gather_start(s)
    for step in list(range(SPLIT, 2 * SPLIT)) + list(range(3 * SPLIT, 4 * SPLIT)):
        tokens_wait(cot, p.t_cot, step)

    fc = p.fc

    def order(step):
        k = lax.rem(step + 1, depth)
        return k, lax.rem(z + k, depth) * 4 * shard

    def early_grads(step, carry):
        k, first = order(step)
        d = at(first, 4 * shard)
        grad_piece(0, first, 4 * shard)[...] = dot_tn(ns[:, d], gg[:, 0 : 2 * fc]).astype(BF16)
        x_copy_of(0, k).start()
        grad_piece(p.cuts, first, 4 * shard)[...] = dot_tn(cot[:, d], ha[:, 0:fc]).astype(BF16)
        x_copy_of(p.cuts, k).start()
        return carry

    def hidden(n):
        lo = p.gather_segs[2 + n][0]

        def step_of(step, carry):
            if n == 0:
                r = tokens_wait(ns, p.t_second, step)
            else:
                _, g, t, h = source(step)
                r = rows_of(g, t, h)
            gate = dot_nn(ns[r, :], w[:, lo : lo + fc])
            up = dot_nn(ns[r, :], w[:, lo + fc : lo + 2 * fc])
            act = dot_nn(cot[r, :], w[:, lo + 2 * fc : lo + 3 * fc])
            sig = 0.5 * jnp.tanh(0.5 * gate) + 0.5
            silu = gate * sig
            ha[r, n * fc : (n + 1) * fc] = (silu * up).astype(BF16)
            gg[r, 2 * n * fc : (2 * n + 1) * fc] = (
                act * up * (sig + silu * (1.0 - sig))
            ).astype(BF16)
            gg[r, (2 * n + 1) * fc : (2 * n + 2) * fc] = (act * silu).astype(BF16)
            return carry

        return step_of

    half = steps // 2
    gather_done(2)
    lax.fori_loop(0, half, hidden(0), 0)
    for n in range(1, p.cuts):
        if n > 1:
            gather_forward(2 + n)
        if n + 1 == p.cuts:
            lax.fori_loop(half, steps, hidden(0), 0)
            for m in range(1, n):
                lax.fori_loop(half, steps, hidden(m), 0)
            hold.wait()
            lax.fori_loop(0, depth, early_grads, 0)
            gather_done(2 + n)
            lax.fori_loop(0, steps, hidden(n), 0)
        else:
            gather_done(2 + n)
            lax.fori_loop(0, half, hidden(n), 0)
    tokens_sent(cot, p.t_cot)
    tokens_sent(ns, p.t_second)
    for s in range(len(p.gather_segs)):
        gather_sent(s)
    keep_send.wait_send()

    def gn2_product(r):
        value = None
        for n, (lo, size) in enumerate(p.gu_segs):
            term = dot_nt(gg[r, 2 * n * fc : (2 * n + 2) * fc], w[:, lo : lo + size])
            value = term if value is None else value + term
        return value

    def set_own(r, value):
        own[r, :] = value

    for h in range(SPLIT):
        over_copy(p.u_out, sy_a, ry_a, h).wait_send()
    partials(p.u_gn2, gn2_product, rd_a, sy_a, ry_a, set_own)

    def grad_gate_up(step, carry):
        k, first = order(step)
        d = at(first, 4 * shard)
        for n in p.kind_gu:
            lo, size = p.sum_segs[n]
            w[d, lo : lo + size] = dot_tn(
                ns[:, d], gg[:, 2 * n * fc : (2 * n + 2) * fc]
            ).astype(BF16)
            x_copy_of(n, k).start()
        return carry

    lax.fori_loop(0, depth, grad_gate_up, 0)
    for k in list(range(1, depth)) + [0]:
        reduce_x(p.kind_early, k)
    for h in range(SPLIT):
        piece = slice(h * part, (h + 1) * part)
        over_copy(p.u_gn2, sy_a, ry_a, h).wait_recv()
        gn2 = own[piece, :] + ry_a[piece, :].astype(F32)
        res = mid_res[piece, :]
        rms = lax.rsqrt(jnp.mean(res * res, axis=1, keepdims=True) + epsilon)
        small_send[0, 1:2, :] += jnp.sum(gn2 * (res * rms), axis=0, keepdims=True)
        q = gn2 * gain1
        value = (
            cot[rows_of(core, y, h), :].astype(F32)
            + rms * q
            - res * (rms * rms * rms) * jnp.mean(q * res, axis=1, keepdims=True)
        )
        own[piece, :] = value
        nfm[rows_of(core, y, h), :] = value.astype(BF16)
        tokens_send(nfm, p.t_mid, h)

    reduce_x(p.kind_gu, 1)

    def blk_product(r):
        value = None
        for n, (lo, size) in enumerate(p.dn_segs):
            term = dot_nt(ha[r, n * fc : (n + 1) * fc], w[:, lo : lo + size])
            value = term if value is None else value + term
        return value

    for h in range(SPLIT):
        over_copy(p.u_gn2, sy_a, ry_a, h).wait_send()
    partials(p.u_blk, blk_product, rd_b, sy_a, ry_b, add_mid, hold=True)
    reduce_x(p.kind_gu, 2)
    restore = local(spilled, ns, p.l_spill)
    restore.start()
    def grad_down(step, carry):
        k, first = order(step)
        d = at(first, 4 * shard)
        for n in p.kind_dn:
            lo, size = p.sum_segs[n]
            first_unit = (n - p.cuts) * fc
            w[d, lo : lo + size] = dot_tn(
                cot[:, d], ha[:, first_unit : first_unit + fc]
            ).astype(BF16)
            x_copy_of(n, k).start()
        return carry

    for n in p.kind_early:
        first = chip * 2 * shard
        grad_piece(n, first, 2 * shard, False)[...] = grad_piece(n, first, 2 * shard)[...]
        for k in range(depth):
            x_copy_of(n, k).wait_send()
        for k in range(1, depth):
            z_copy_of(n, k).wait_send()
    proj_back = local(proj_held, proj, p.l_proj)
    proj_back.start()
    lax.fori_loop(0, depth, grad_down, 0)
    for k in range(3, depth):
        reduce_x(p.kind_gu, k)

    grow = group
    gcol = p.cq

    def grad_mixer(step, carry):
        r = tokens_wait(nfm, p.t_mid, step)
        _, g, t, h = source(step)
        value = dot_nn(nfm[r, :], w[:, 3 * p.cq : p.mix]).astype(BF16)
        rr = at(grow + t * rows + h * part, part)

        @pl.when(g == 0)
        def _():
            gg[rr, 0:gcol] = value

        @pl.when(g == 1)
        def _():
            gg[rr, gcol : 2 * gcol] = value

        return carry

    lax.fori_loop(0, steps, grad_mixer, 0)
    for h in range(SPLIT):
        over_copy(p.u_blk, sy_a, ry_b, h).start()

    def conv_backward(step, carry):
        g = jnp.where(step // lanes == 0, 1 - core, core)
        j = step % lanes
        r, col, b, c, xv, k1, k2, t, gated, d1, d2, conv = conv_terms(g, j)
        gm = gg[grow : 2 * grow, pl.ds(pl.multiple_of(g * gcol + j * 128, 128), 128)].astype(F32)
        gco = gm * c
        grad_gated = (
            t[0:1] * gco
            + t[1:2] * pltpu.roll(gco * k1, group - 1, 0)
            + t[2:3] * pltpu.roll(gco * k2, group - 2, 0)
        )
        place = pl.ds(pl.multiple_of((y * 2 + core) * p.cq + j * 128, 128), 128)
        for n, term in enumerate((gated, d1, d2)):
            small_send[0, 8 + n : 9 + n, place] += jnp.sum(gco * term, axis=0, keepdims=True)
        proj[r, pl.ds(col, 128)] = (grad_gated * xv).astype(BF16)
        proj[r, pl.ds(pl.multiple_of(col + p.cq, 128), 128)] = (gm * conv).astype(BF16)
        proj[r, pl.ds(pl.multiple_of(col + 2 * p.cq, 128), 128)] = (grad_gated * b).astype(BF16)
        return carry

    proj_back.wait()
    lax.fori_loop(0, 2 * lanes, conv_backward, 0)
    restore.wait()
    x_back = local(x_in, ha.at[rows:group, 0:width], p.l_x)
    x_back.start()
    mx0 = p.kind_mix[0]

    def grad_mix(step, carry):
        k, first = order(step)
        d = at(first, 4 * shard)
        place = at(group + first, 4 * shard)
        ha[place, 0 : 3 * p.cq] = dot_tn(ns[:, d], proj[...]).astype(BF16)
        ha[place, 3 * p.cq : p.mix] = dot_tn(nfm[:, d], mix[...]).astype(BF16)
        x_copy_of(mx0, k).start()
        return carry

    lax.fori_loop(0, depth, grad_mix, 0)
    reduce_x(p.kind_gu, 0)

    def block_output():
        for k in list(range(1, depth)) + [0]:
            reduce_x(p.kind_dn, k)
        for h in range(SPLIT):
            piece = slice(h * part, (h + 1) * part)
            over_copy(p.u_blk, sy_a, ry_b, h).wait_recv()
            ha[piece, 0:width] = (mid_res[piece, :] + ry_b[piece, :].astype(F32)).astype(BF16)
        local(ha.at[0:rows, 0:width], blk_out, p.l_blk).start()

    def gain_sum(r, value):
        small_send[0, 0:1, :] += jnp.sum(value * ns[r, :].astype(F32), axis=0, keepdims=True)

    def set_mid(r, value):
        mid_res[r, :] = value

    partials(
        p.u_gn1,
        lambda r: dot_nt(proj[r, :], w[:, 0 : 3 * p.cq]),
        rd_a, rd_b, ry_a, set_mid, between=block_output, observe=gain_sum,
    )
    small_copy(0).start()
    reduce_x(p.kind_mix, 1)
    small_step(0)
    small_copy(1).start()
    reduce_x(p.kind_mix, 2)
    small_step(1)
    small_copy(2).start()
    for k in list(range(3, depth)) + [0]:
        reduce_x(p.kind_mix, k)
    small_step(2)
    for k in range(1, depth):
        small_copy(3, k).start()
    x_back.wait()
    for h in range(SPLIT):
        piece = slice(h * part, (h + 1) * part)
        over_copy(p.u_gn1, rd_b, ry_a, h).wait_recv()
        gn1 = mid_res[piece, :] + ry_a[piece, :].astype(F32)
        xf = ha[rows + h * part : rows + (h + 1) * part, 0:width].astype(F32)
        rms = lax.rsqrt(jnp.mean(xf * xf, axis=1, keepdims=True) + epsilon)
        q = gn1 * gain0
        if h == 0:
            local(ha.at[0:rows, 0:width], blk_out, p.l_blk).wait()
        ha[piece, 0:width] = (
            own[piece, :]
            + rms * q
            - xf * (rms * rms * rms) * jnp.mean(q * xf, axis=1, keepdims=True)
        ).astype(BF16)
    tok_copy = local(ha.at[0:rows, 0:width], tok_out, p.l_tok)
    tok_copy.start()

    reduce_z(p.kind_early)
    reduce_z(p.kind_gu)
    reduce_core(p.kind_early)
    reduce_z(p.kind_dn)
    reduce_core(p.kind_gu)
    reduce_z(p.kind_mix)
    reduce_core(p.kind_dn)
    total = small_send[3]
    for k in range(1, depth):
        small_copy(3, k).wait_recv()
        total = total + small_recv[3 + k - 1]
    sums_out[...] = total
    sums_out[0:1, :] = total[0:1, :] / gain0
    reduce_core(p.kind_mix)
    for n in range(len(p.sum_segs)):
        for c in out_copies(n, 0) + out_copies(n, 1):
            c.wait()
    tok_copy.wait()
    for h in range(SPLIT):
        over_copy(p.u_blk, sy_a, ry_b, h).wait_send()
    tokens_sent(nfm, p.t_mid)
    for h in range(SPLIT):
        over_copy(p.u_gn1, rd_b, ry_a, h).wait_send()
    for n in range(len(p.sum_segs)):
        if n not in p.kind_early:
            for k in range(depth):
                x_copy_of(n, k).wait_send()
            for k in range(1, depth):
                z_copy_of(n, k).wait_send()
        c_copy_of(n).wait_send()
    for n in range(3):
        small_copy(n).wait_send()
    for k in range(1, depth):
        small_copy(3, k).wait_send()


def fused_body(depth, tokens, cotangent, lengths, w_in, w_out, w_gate_up, w_down, conv_weight, norm_gains):
    rows, width = tokens.shape
    shard, taken, chan = w_in.shape
    hidden = w_gate_up.shape[2]
    plan = Plan(depth, rows, width, shard, chan, hidden)
    if plan.cuts < 3 or plan.width > 2 * rows or (2 * plan.cuts + 1) * shard > rows:
        return body(
            tokens, cotangent, lengths, w_in, w_out, w_gate_up, w_down, conv_weight, norm_gains
        )
    cq = plan.cq
    total = 4 * rows
    any_spec = pl.BlockSpec(memory_space=pl.ANY)
    vmem_spec = pl.BlockSpec(memory_space=pltpu.VMEM)
    shape = jax.ShapeDtypeStruct
    outs = (
        shape((rows, width), BF16),
        shape((rows, width), BF16),
        shape((taken, shard, chan), F32),
        shape((shard, chan), F32),
        shape((2, shard, hidden), F32),
        shape((shard, hidden), F32),
        shape((16, width), F32),
        shape((depth, 2 * shard, plan.cols), BF16),
        shape((depth - 1, 2 * shard, plan.cols), BF16),
        shape((total, width), BF16),
        shape((total, 3 * cq), BF16),
    )
    vm = pltpu.VMEM
    block_out, grad_tokens, grad_in, grad_out, grad_gu, grad_dn, sums, _, _, _, _ = pl.pallas_call(
        functools.partial(block_kernel, plan),
        out_shape=outs,
        in_specs=[
            any_spec, any_spec, pl.BlockSpec(memory_space=pltpu.SMEM),
            any_spec, any_spec, any_spec, any_spec, vmem_spec, vmem_spec,
        ],
        out_specs=(any_spec,) * 6 + (vmem_spec,) + (any_spec,) * 4,
        scratch_shapes=[
            vm((width, plan.cols), BF16),
            vm((total, width), BF16),
            vm((total, width), BF16),
            vm((total, width), BF16),
            vm((total, 3 * cq), BF16),
            vm((total, 2 * plan.fq), BF16),
            vm((total, plan.fq), BF16),
            vm((total, cq), BF16),
            vm((2 * rows, width), BF16),
            vm((2 * rows, width), BF16),
            vm((rows, width), BF16),
            vm((rows, width), BF16),
            vm((2 * rows, width), BF16),
            vm((rows, width), BF16),
            vm((rows, width), F32),
            vm((rows, width), F32),
            vm((shard, plan.cols), BF16),
            vm((2, 2 * rows, 256), BF16),
            vm((4, 16, width), F32),
            vm((3 + depth - 1, 16, width), F32),
            pltpu.SemaphoreType.DMA((plan.remote,)),
            pltpu.SemaphoreType.DMA((plan.remote,)),
            pltpu.SemaphoreType.DMA((plan.local,)),
        ],
        compiler_params=pltpu.CompilerParams(
            collective_id=0, has_side_effects=True, vmem_limit_bytes=63 * 2**20
        ),
    )(
        tokens, cotangent, lengths, w_in.transpose(1, 0, 2), w_out.T, w_gate_up.transpose(1, 0, 2),
        w_down.T, conv_weight, norm_gains,
    )
    y = lax.axis_index("tensor")
    grad_taps = lax.dynamic_slice(sums, (8, y * chan), (conv_weight.shape[0], chan))
    return (
        block_out,
        grad_tokens,
        grad_in.transpose(1, 0, 2),
        grad_out.T,
        grad_gu.transpose(1, 0, 2),
        grad_dn.T,
        grad_taps,
        sums[:2],
    )


def solution(mesh):
    dp, tensor = mesh.shape["dp"], mesh.shape["tensor"]
    grouped = tensor == 2 and dp == 16
    return jax.shard_map(
        functools.partial(fused_body, dp // 4) if grouped else body,
        mesh=mesh,
        in_specs=(
            P(("dp", "tensor"), None),
            P(("dp", "tensor"), None),
            P("dp", None),
            P("dp", None, "tensor"),
            P("tensor", "dp"),
            P("dp", None, "tensor"),
            P("tensor", "dp"),
            P(None, "tensor"),
            P(),
        ),
        out_specs=(
            P(("dp", "tensor"), None),
            P(("dp", "tensor"), None),
            P("dp", None, "tensor"),
            P("tensor", "dp"),
            P("dp", None, "tensor"),
            P("tensor", "dp"),
            P(None, "tensor"),
            P(),
        ),
        check_vma=False,
    )
```

```python
import functools

import jax
import jax.numpy as jnp
from jax import lax
from jax.experimental import pallas as pl
from jax.experimental.pallas import tpu as pltpu
from jax.sharding import PartitionSpec as P

epsilon = 1e-05


def sequence_starts(seq_lengths):
    count = seq_lengths.shape[0]
    before = jnp.arange(count)[None, :] < jnp.arange(count)[:, None]
    return jnp.sum(jnp.where(before, seq_lengths[None, :], 0), axis=1)


def positions(seq_lengths, row_count):
    starts = sequence_starts(seq_lengths)
    row_index = jnp.arange(row_count, dtype=jnp.int32)
    begun_at = jnp.where(starts[None, :] <= row_index[:, None], starts[None, :], jnp.int32(0))
    return row_index - jnp.max(begun_at, axis=1)


def delayed(values, steps):
    return jnp.concatenate([jnp.zeros((steps, values.shape[1]), values.dtype), values[:-steps]], 0)


def advanced(values, steps):
    return jnp.concatenate([values[steps:], jnp.zeros((steps, values.shape[1]), values.dtype)], 0)


def gather_rows(values):
    count = lax.axis_size("tensor")
    if count != 2:
        return lax.all_gather(values, "tensor", axis=0, tiled=True)
    rows = values.shape[0]
    index = lax.axis_index("tensor")
    other = lax.ppermute(values, "tensor", [(0, 1), (1, 0)])
    whole = jnp.zeros((2 * rows, values.shape[1]), values.dtype)
    whole = lax.dynamic_update_slice_in_dim(whole, values, index * rows, 0)
    return lax.dynamic_update_slice_in_dim(whole, other, (1 - index) * rows, 0)


def scatter_rows(values):
    count = lax.axis_size("tensor")
    if count != 2:
        return lax.psum_scatter(
            values.astype(jnp.bfloat16), "tensor", scatter_dimension=0, tiled=True
        ).astype(jnp.float32)
    rows = values.shape[0] // 2
    index = lax.axis_index("tensor")
    away = lax.dynamic_slice_in_dim(values, (1 - index) * rows, rows, 0).astype(jnp.bfloat16)
    other = lax.ppermute(away, "tensor", [(0, 1), (1, 0)])
    return lax.dynamic_slice_in_dim(values, index * rows, rows, 0) + other.astype(jnp.float32)


def butterfly_sum(values, axis):
    count = lax.axis_size(axis)
    if count & (count - 1):
        return lax.psum(values, axis)
    step = 1
    while step < count:
        values = values + lax.ppermute(values, axis, [(i, i ^ step) for i in range(count)])
        step *= 2
    return values


def gather_blocks(shard, axis):
    count = lax.axis_size(axis)
    if count & (count - 1):
        return lax.all_gather(shard, axis, axis=0, tiled=True)
    index = lax.axis_index(axis)
    blocks = shard[None]
    step = count // 2
    while step >= 1:
        other = lax.ppermute(blocks, axis, [(i, i ^ step) for i in range(count)])
        upper = (index // step) % 2 == 1
        first = jnp.where(upper, other, blocks)
        second = jnp.where(upper, blocks, other)
        blocks = jnp.stack([first, second], axis=1).reshape((-1,) + shard.shape)
        step //= 2
    return blocks.reshape((-1,) + shard.shape[1:])


def scatter_blocks(values, axis):
    count = lax.axis_size(axis)
    if count & (count - 1):
        return lax.psum_scatter(values, axis, scatter_dimension=0, tiled=True)
    index = lax.axis_index(axis)
    shape = (values.shape[0] // count,) + values.shape[1:]
    step = 1
    while step < count:
        pairs = values.reshape((count // step // 2, 2) + shape)
        side = (index // step) % 2
        away = lax.dynamic_index_in_dim(pairs, 1 - side, 1, keepdims=False)
        kept = lax.dynamic_index_in_dim(pairs, side, 1, keepdims=False)
        other = lax.ppermute(away, axis, [(i, i ^ step) for i in range(count)])
        values = (kept.astype(jnp.float32) + other.astype(jnp.float32)).astype(values.dtype)
        step *= 2
    return values.reshape(shape)


def body(tokens, cotangent, lengths, w_in, w_out, w_gate_up, w_down, conv_weight, norm_gains):
    shard_rows, taken, chan_count = w_in.shape
    hidden = w_gate_up.shape[2]
    packed = jnp.concatenate([w_in.reshape(shard_rows, taken * chan_count), w_out.T], axis=1)
    full_mix = lax.all_gather(packed, "dp", axis=0, tiled=True)
    full_gu = lax.all_gather(
        w_gate_up.reshape(shard_rows, 2 * hidden), "dp", axis=0, tiled=True
    )
    full_down = gather_blocks(w_down.T, "dp")
    full_in = full_mix[:, : taken * chan_count]
    full_out = full_mix[:, taken * chan_count :]
    x_float = tokens.astype(jnp.float32)
    rms_first = lax.rsqrt(jnp.mean(x_float * x_float, axis=1, keepdims=True) + epsilon)
    normed_first = (x_float * rms_first * norm_gains[0]).astype(jnp.bfloat16)
    first_all = gather_rows(normed_first)
    cot_all = gather_rows(cotangent)
    row_count = first_all.shape[0]
    position = positions(lengths[0], row_count)
    first_keep = (position >= 1).astype(jnp.float32)[:, None]
    second_keep = (position >= 2).astype(jnp.float32)[:, None]
    projected = jnp.dot(first_all, full_in, preferred_element_type=jnp.float32)
    proj_b = projected[:, :chan_count]
    proj_c = projected[:, chan_count : 2 * chan_count]
    proj_x = projected[:, 2 * chan_count :]
    gated_in = proj_b * proj_x
    conv_out = (
        conv_weight[0] * gated_in
        + conv_weight[1] * delayed(gated_in, 1) * first_keep
        + conv_weight[2] * delayed(gated_in, 2) * second_keep
    )
    mixer_in = (proj_c * conv_out).astype(jnp.bfloat16)
    residual_mid = x_float + scatter_rows(
        jnp.einsum("rc,dc->rd", mixer_in, full_out, preferred_element_type=jnp.float32)
    )
    rms_second = lax.rsqrt(jnp.mean(residual_mid * residual_mid, axis=1, keepdims=True) + epsilon)
    normed_second = (residual_mid * rms_second * norm_gains[1]).astype(jnp.bfloat16)
    second_all = gather_rows(normed_second)
    gate_up = jnp.dot(second_all, full_gu, preferred_element_type=jnp.float32)
    gate_pre = gate_up[:, :hidden]
    up_pre = gate_up[:, hidden:]
    sig_gate = jax.nn.sigmoid(gate_pre)
    hidden_act = (gate_pre * sig_gate * up_pre).astype(jnp.bfloat16)
    grad_down = jnp.einsum("rd,rf->df", cot_all, hidden_act, preferred_element_type=jnp.float32)
    grad_down, full_down = lax.optimization_barrier((grad_down.astype(jnp.bfloat16), full_down))
    sum_down = lax.psum_scatter(grad_down, "dp", scatter_dimension=0, tiled=True)
    grad_act = jnp.einsum("rd,df->rf", cot_all, full_down, preferred_element_type=jnp.float32)
    grad_gate = (grad_act * up_pre * sig_gate * (1.0 + gate_pre * (1.0 - sig_gate))).astype(
        jnp.bfloat16
    )
    grad_up = (grad_act * gate_pre * sig_gate).astype(jnp.bfloat16)
    grad_hidden = jnp.concatenate([grad_gate, grad_up], axis=1)
    grad_gu = jnp.einsum("rd,rf->df", second_all, grad_hidden, preferred_element_type=jnp.float32)
    grad_gu, grad_gate, grad_up = lax.optimization_barrier(
        (grad_gu.astype(jnp.bfloat16), grad_gate, grad_up)
    )
    grad_hidden = jnp.concatenate([grad_gate, grad_up], axis=1)
    grad_gu, sum_down = lax.optimization_barrier((grad_gu, sum_down))
    sum_gu = lax.psum_scatter(grad_gu, "dp", scatter_dimension=0, tiled=True)
    grad_normed2 = scatter_rows(
        jnp.einsum("rf,df->rd", grad_hidden, full_gu, preferred_element_type=jnp.float32)
    )
    block_out = (
        residual_mid
        + scatter_rows(
            jnp.einsum("rf,df->rd", hidden_act, full_down, preferred_element_type=jnp.float32)
        )
    ).astype(jnp.bfloat16)
    scaled_two = grad_normed2 * norm_gains[1]
    grad_mid = (
        cotangent.astype(jnp.float32)
        + rms_second * scaled_two
        - residual_mid
        * (rms_second * rms_second * rms_second)
        * jnp.mean(scaled_two * residual_mid, axis=1, keepdims=True)
    )
    gain_two = jnp.sum(grad_normed2 * residual_mid * rms_second, axis=0)
    mid_all = gather_rows(grad_mid.astype(jnp.bfloat16))
    grad_mixer_in = jnp.dot(mid_all, full_out, preferred_element_type=jnp.float32)
    grad_wout = jnp.einsum("rd,rc->dc", mid_all, mixer_in, preferred_element_type=jnp.float32)
    grad_conv_out = grad_mixer_in * proj_c
    grad_gated = (
        conv_weight[0] * grad_conv_out
        + conv_weight[1] * advanced(grad_conv_out * first_keep, 1)
        + conv_weight[2] * advanced(grad_conv_out * second_keep, 2)
    )
    grad_taps = jnp.stack(
        [
            jnp.sum(grad_conv_out * gated_in, axis=0),
            jnp.sum(grad_conv_out * first_keep * delayed(gated_in, 1), axis=0),
            jnp.sum(grad_conv_out * second_keep * delayed(gated_in, 2), axis=0),
        ]
    )
    grad_proj = jnp.concatenate(
        [grad_gated * proj_x, grad_mixer_in * conv_out, grad_gated * proj_b], axis=1
    ).astype(jnp.bfloat16)
    grad_win = jnp.einsum("rd,rf->df", first_all, grad_proj, preferred_element_type=jnp.float32)
    grad_mix = jnp.concatenate(
        [grad_win.astype(jnp.bfloat16), grad_wout.astype(jnp.bfloat16)], axis=1
    )
    sum_mix = scatter_blocks(grad_mix, "dp")
    grad_normed1 = scatter_rows(
        jnp.einsum("rf,df->rd", grad_proj, full_in, preferred_element_type=jnp.float32)
    )
    scaled_one = grad_normed1 * norm_gains[0]
    grad_tokens = (
        grad_mid
        + rms_first * scaled_one
        - x_float
        * (rms_first * rms_first * rms_first)
        * jnp.mean(scaled_one * x_float, axis=1, keepdims=True)
    ).astype(jnp.bfloat16)
    gain_one = jnp.sum(grad_normed1 * x_float * rms_first, axis=0)
    model_width = tokens.shape[1]
    sums = butterfly_sum(
        jnp.concatenate([gain_one, gain_two, grad_taps.reshape(-1)]).reshape(-1, 128), "dp"
    ).reshape(-1)
    gain_sums = butterfly_sum(sums[: 2 * model_width].reshape(2, model_width), "tensor")
    grad_conv = sums[2 * model_width :].reshape(grad_taps.shape)
    split = taken * chan_count
    shard_in = sum_mix[:, :split].astype(jnp.float32).reshape(w_in.shape)
    shard_out = sum_mix[:, split:].astype(jnp.float32).T
    shard_gu = sum_gu.astype(jnp.float32).reshape(w_gate_up.shape)
    shard_down = sum_down.astype(jnp.float32).T
    return (block_out, grad_tokens, shard_in, shard_out, shard_gu, shard_down, grad_conv, gain_sums)


MESH = pl.DeviceIdType.MESH
F32 = jnp.float32
BF16 = jnp.bfloat16
SPLIT = 2


def dot_nn(a, b):
    return jnp.dot(a, b, preferred_element_type=F32)


def dot_nt(a, b):
    return lax.dot_general(a, b, (((1,), (1,)), ((), ())), preferred_element_type=F32)


def dot_tn(a, b):
    return lax.dot_general(a, b, (((0,), (0,)), ((), ())), preferred_element_type=F32)


class Slots:
    def __init__(self):
        self.count = 0

    def take(self, number):
        first = self.count
        self.count += number
        return first


class Plan:
    def __init__(self, depth, rows, width, shard, chan, hidden):
        self.depth, self.rows, self.width, self.shard = depth, rows, width, shard
        self.cq, self.fq = chan // 2, hidden // 2
        self.cuts = 3 if self.fq % 384 == 0 else 1
        self.fc = self.fq // self.cuts
        self.part = rows // SPLIT
        cq, fc = self.cq, self.fc
        self.mix = 4 * cq
        self.cols = self.mix + 3 * self.fq
        self.gather_segs = [(0, 3 * cq), (3 * cq, cq)] + [
            (self.mix + 3 * fc * n, 3 * fc) for n in range(self.cuts)
        ]
        self.gu_segs = [(self.mix + 3 * fc * n, 2 * fc) for n in range(self.cuts)]
        self.dn_segs = [(self.mix + 3 * fc * n + 2 * fc, fc) for n in range(self.cuts)]
        self.mix_segs = [(0, self.mix)]
        self.sum_segs = self.gu_segs + self.dn_segs + self.mix_segs
        self.kind_early = [0, self.cuts]
        self.kind_gu = list(range(1, self.cuts))
        self.kind_dn = list(range(self.cuts + 1, 2 * self.cuts))
        self.kind_mix = [2 * self.cuts]
        s = Slots()
        self.pieces = [
            [("in", k, 0, k * cq, cq) for k in range(3)],
            [("out", 0, 0, 3 * cq, cq)],
        ] + [
            [("gu", k, n * fc, self.mix + (3 * n + k) * fc, fc) for k in range(2)]
            + [("dn", 0, n * fc, self.mix + (3 * n + 2) * fc, fc)]
            for n in range(self.cuts)
        ]
        self.g_core = [s.take(len(pieces)) for pieces in self.pieces]
        self.g_z = [s.take(depth - 1) for _ in self.gather_segs]
        self.g_x = [s.take(depth) for _ in self.gather_segs]
        self.g_on = [s.take(depth - 1) for _ in self.gather_segs]
        self.t_first, self.t_cot, self.t_second, self.t_mid = [s.take(3 * SPLIT) for _ in range(4)]
        self.u_out, self.u_gn2, self.u_blk, self.u_gn1 = [s.take(3 * SPLIT) for _ in range(4)]
        self.r_x = [s.take(depth) for _ in self.sum_segs]
        self.r_z = [s.take(depth - 1) for _ in self.sum_segs]
        self.r_c = [s.take(1) for _ in self.sum_segs]
        self.keep = s.take(1)
        self.small = s.take(3 + depth - 1)
        self.remote = s.count
        s = Slots()
        self.l_gather = [s.take(len(pieces)) for pieces in self.pieces]
        self.l_x, self.l_cot, self.l_spill, self.l_proj = [s.take(1) for _ in range(4)]
        self.l_xr, self.l_zr = s.take(self.cuts), s.take(self.cuts * (depth - 1))
        self.l_out = [s.take(2 * 4) for _ in self.sum_segs]
        self.l_blk, self.l_tok = s.take(1), s.take(1)
        self.local = s.count


def block_kernel(
    plan, x_in, cot_in, lengths, in_in, out_in, gu_in, dn_in, taps_in, gains,
    blk_out, tok_out, in_out, out_out, gu_out, dn_out, taps_out, sums_out, xr, zr, spilled, proj_held,
    w, nfm, ns, cot, proj, gg, ha, mix, rd_a, rd_b, ry_a, ry_b, sd, sy_a,
    own, mid_res, cr, keep, small_send, small_recv,
    ssem, rsem, lsem,
):
    p = plan
    depth, rows, part, shard, width = p.depth, p.rows, p.part, p.shard, p.width
    group = 2 * rows
    i = lax.axis_index("dp")
    y = lax.axis_index("tensor")
    core = lax.rem(i, 2)
    chip = i // 2
    x = lax.rem(chip, 2)
    z = chip // 2
    sib = (i + 1 - 2 * core, y)
    over = (i, 1 - y)
    aside = (i + 2 - 4 * x, y)

    def along(k):
        return (lax.rem(z + k, depth) * 4 + x * 2 + core, y)

    def sender(k):
        return lax.rem(z - k + depth, depth)

    def at(first, size):
        return pl.ds(pl.multiple_of(first, size), size)

    def remote(src, dst, slot, device):
        return pltpu.make_async_remote_copy(
            src_ref=src, dst_ref=dst, send_sem=ssem.at[slot], recv_sem=rsem.at[slot],
            device_id=device, device_id_type=MESH,
        )

    def local(src, dst, slot):
        return pltpu.make_async_copy(src, dst, lsem.at[slot])

    barrier = pltpu.get_barrier_semaphore()
    partners = [sib, over, aside] + [along(k) for k in range(1, depth)]
    for device in partners:
        pl.semaphore_signal(barrier, inc=1, device_id=device, device_id_type=MESH)
    x_copy = local(x_in, ry_b, p.l_x)
    x_copy.start()
    mine = at(i * shard, shard)

    def shard_piece(piece, for_core):
        name, index, first, lo, size = piece
        share = p.cq if name in ("in", "out") else p.fq
        col = pl.ds(pl.multiple_of(for_core * share + first, 128), size)
        if name == "in":
            return in_in.at[index, :, col], w.at[mine, lo : lo + size]
        if name == "gu":
            return gu_in.at[index, :, col], w.at[mine, lo : lo + size]
        return (out_in if name == "out" else dn_in).at[:, col], w.at[mine, lo : lo + size]

    gather_local = [
        [local(*shard_piece(piece, core), p.l_gather[s] + n) for n, piece in enumerate(pieces)]
        for s, pieces in enumerate(p.pieces)
    ]
    for copies in gather_local:
        for c in copies:
            c.start()
    slot0 = (core * 2 + y) * rows
    cot_local = local(cot_in, cot.at[at(slot0, rows), :], p.l_cot)
    cot_local.start()
    pl.semaphore_wait(barrier, len(partners))

    core_sends = [
        [
            remote(*shard_piece(piece, 1 - core), p.g_core[s] + n, sib)
            for n, piece in enumerate(pieces)
        ]
        for s, pieces in enumerate(p.pieces)
    ]
    keep_send = remote(keep.at[core], keep.at[core], p.keep, sib)

    def chip_block(zz, xx):
        return at((zz * 2 + xx) * 2 * shard, 2 * shard)

    def own_block(s):
        lo, size = p.gather_segs[s]
        return w.at[chip_block(z, x), lo : lo + size]

    def gather_z(s, k):
        return remote(own_block(s), own_block(s), p.g_z[s] + k - 1, along(k))

    def gather_x(s, k):
        lo, size = p.gather_segs[s]
        piece = w.at[chip_block(sender(k), x), lo : lo + size]
        return remote(piece, piece, p.g_x[s] + k, aside)

    line = depth == 4

    def direct(k):
        return {1: z != 3, 2: (z == 0) | (z == 3), 3: z != 0}[k] if line else k > 0

    def onward(k):
        return {1: z == 2, 2: (z == 1) | (z == 2), 3: z == 1}[k]

    def gather_on(s, k):
        lo, size = p.gather_segs[s]
        piece = w.at[chip_block(sender(k), x), lo : lo + size]
        end = jnp.where(z == 1, 0, 3)
        arrives = p.g_z[s] + lax.rem(end - z + k + depth, depth) - 1
        return pltpu.make_async_remote_copy(
            src_ref=piece, dst_ref=piece, send_sem=ssem.at[p.g_on[s] + k - 1],
            recv_sem=rsem.at[arrives], device_id=(end * 4 + x * 2 + core, y), device_id_type=MESH,
        )

    def gather_start(s):
        for c in gather_local[s]:
            c.wait()
        for c in core_sends[s]:
            c.wait_recv()
        for k in range(1, depth):

            @pl.when(direct(k))
            def _(k=k):
                gather_z(s, k).start()

        gather_x(s, 0).start()

    def gather_forward(s):
        for k in [3, 1, 2] if line else range(1, depth):
            gather_z(s, k).wait_recv()
            if line:

                @pl.when(onward(k))
                def _(k=k):
                    gather_on(s, k).start()

            gather_x(s, k).start()

    def gather_done(s):
        for k in range(depth):
            gather_x(s, k).wait_recv()

    def gather_sent(s):
        for k in range(1, depth):

            @pl.when(direct(k))
            def _(k=k):
                gather_z(s, k).wait_send()

            if line:

                @pl.when(onward(k))
                def _(k=k):
                    gather_on(s, k).wait_send()

        for k in range(depth):
            gather_x(s, k).wait_send()
        for c in core_sends[s]:
            c.wait_send()

    def rows_of(g, t, h):
        return at((g * 2 + t) * rows + h * part, part)

    def token_copy(buffer, base, kind, h):
        g, t = (core, y) if kind < 2 else (core, 1 - y)
        device = over if kind == 1 else sib
        piece = buffer.at[rows_of(g, t, h), :]
        return remote(piece, piece, base + kind * SPLIT + h, device)

    def tokens_send(buffer, base, h):
        token_copy(buffer, base, 1, h).start()
        token_copy(buffer, base, 0, h).start()

    def tokens_sent(buffer, base):
        for h in range(SPLIT):
            for kind in range(3):
                token_copy(buffer, base, kind, h).wait_send()

    def source(step):
        kind = step // SPLIT
        g = jnp.where(kind % 2 == 0, core, 1 - core)
        t = jnp.where(kind // 2 == 0, y, 1 - y)
        return kind, g, t, step % SPLIT

    def tokens_wait(buffer, base, step):
        kind, g, t, h = source(step)

        @pl.when(kind > 0)
        def _():
            piece = buffer.at[rows_of(g, t, h), :]
            remote(piece, piece, base + (kind - 1) * SPLIT + h, sib).wait_recv()

        @pl.when(kind == 2)
        def _():
            piece = buffer.at[rows_of(g, t, h), :]
            remote(piece, piece, base + 2 * SPLIT + h, sib).start()

        return rows_of(g, t, h)

    steps = 4 * SPLIT

    def core_copy(base, recv, q):
        piece = at(q * part, part)
        return remote(sd.at[piece, :], recv.at[piece, :], base + q, sib)

    def over_copy(base, send, recv, h):
        piece = at(h * part, part)
        return remote(send.at[piece, :], recv.at[piece, :], base + 2 * SPLIT + h, over)

    def partials(base, product, recv, send, recv_over, keep_own, hold=False, between=None, observe=None):
        def to_sibling(q, carry):
            t, h = jnp.where(q // SPLIT == 0, 1 - y, y), q % SPLIT
            n = t * SPLIT + h
            value = product(rows_of(1 - core, t, h))
            if observe:
                observe(rows_of(1 - core, t, h), value)
            sd[at(n * part, part), :] = value.astype(BF16)
            core_copy(base, recv, n).start()
            return carry

        lax.fori_loop(0, 2 * SPLIT, to_sibling, 0)

        def to_over(h, carry):
            n = (1 - y) * SPLIT + h
            value = product(rows_of(core, 1 - y, h))
            if observe:
                observe(rows_of(core, 1 - y, h), value)
            core_copy(base, recv, n).wait_recv()
            value = value + recv[at(n * part, part), :].astype(F32)
            send[at(h * part, part), :] = value.astype(BF16)
            if not hold:
                over_copy(base, send, recv_over, h).start()
            return carry

        lax.fori_loop(0, SPLIT, to_over, 0)
        if between:
            between()

        def to_own(h, carry):
            n = y * SPLIT + h
            value = product(rows_of(core, y, h))
            if observe:
                observe(rows_of(core, y, h), value)
            core_copy(base, recv, n).wait_recv()
            keep_own(at(h * part, part), value + recv[at(n * part, part), :].astype(F32))
            return carry

        lax.fori_loop(0, SPLIT, to_own, 0)
        for q in range(2 * SPLIT):
            core_copy(base, recv, q).wait_send()

    def grad_piece(n, first, size, early=True):
        lo, cols = p.sum_segs[n]
        if early and n in p.kind_early:
            base = 0 if n < p.cuts else width
            return proj.at[at(base + first, size), 0:cols]
        if n in p.kind_mix:
            return ha.at[at(group + first, size), 0:cols]
        return w.at[at(first, size), lo : lo + cols]

    def x_copy_of(n, k):
        lo, size = p.sum_segs[n]
        zz = lax.rem(z + k, depth)
        piece = grad_piece(n, (zz * 2 + 1 - x) * 2 * shard, 2 * shard)
        return remote(piece, xr.at[k, :, lo : lo + size], p.r_x[n] + k, aside)

    def z_copy_of(n, k):
        lo, size = p.sum_segs[n]
        zz = lax.rem(z + k, depth)
        piece = grad_piece(n, (zz * 2 + x) * 2 * shard, 2 * shard)
        return remote(piece, zr.at[k - 1, :, lo : lo + size], p.r_z[n] + k - 1, along(k))

    def c_copy_of(n):
        lo, size = p.sum_segs[n]
        piece = grad_piece(n, (i + 1 - 2 * core) * shard, shard, False)
        return remote(piece, cr.at[:, lo : lo + size], p.r_c[n], sib)

    def stage_place(kind, which, n, rank):
        number = kind.index(n)
        if kind is p.kind_early and which == "x":
            return sd, number * 2 * shard, 0
        return gg, rank * 2 * shard, sum(p.sum_segs[m][1] for m in kind[:number])

    def staged(kind, which, n, k):
        lo, size = p.sum_segs[n]
        number = kind.index(n)
        buffer, row, col = stage_place(kind, which, n, 0 if which == "x" else k)
        dst = buffer.at[row : row + 2 * shard, col : col + size]
        if which == "x":
            return local(xr.at[k, :, lo : lo + size], dst, p.l_xr + number)
        slot = p.l_zr + number * (depth - 1) + k - 1
        return local(zr.at[k - 1, :, lo : lo + size], dst, slot)

    def reduce_x(kind, k):
        zz = lax.rem(z + k, depth)
        for n in kind:
            x_copy_of(n, k).wait_recv()
            staged(kind, "x", n, k).start()
        for n in kind:
            size = p.sum_segs[n][1]
            buffer, row, col = stage_place(kind, "x", n, 0)
            staged(kind, "x", n, k).wait()
            piece = grad_piece(n, (zz * 2 + x) * 2 * shard, 2 * shard)
            piece[...] = (
                piece[...].astype(F32)
                + buffer[row : row + 2 * shard, col : col + size].astype(F32)
            ).astype(BF16)
            if k:
                z_copy_of(n, k).start()

    def out_copies(n, which):
        buffer, place = ((own, core), (mid_res, 1 - core))[which]
        held = slice(n * shard, (n + 1) * shard)
        if n < p.cuts:
            col = pl.ds(pl.multiple_of(place * p.fq + n * p.fc, 128), p.fc)
            parts = [(k * p.fc, p.fc, gu_out.at[k, :, col]) for k in range(2)]
        elif n < 2 * p.cuts:
            col = pl.ds(pl.multiple_of(place * p.fq + (n - p.cuts) * p.fc, 128), p.fc)
            parts = [(0, p.fc, dn_out.at[:, col])]
        else:
            col = pl.ds(pl.multiple_of(place * p.cq, 128), p.cq)
            parts = [(k * p.cq, p.cq, in_out.at[k, :, col]) for k in range(3)]
            parts.append((3 * p.cq, p.cq, out_out.at[:, col]))
        return [
            local(buffer.at[held, lo : lo + size], dst, p.l_out[n] + which * 4 + number)
            for number, (lo, size, dst) in enumerate(parts)
        ]

    def reduce_z(kind):
        for n in kind:
            for k in range(1, depth):
                z_copy_of(n, k).wait_recv()
                staged(kind, "z", n, k).start()
        for n in kind:
            size = p.sum_segs[n][1]
            for k in range(1, depth):
                staged(kind, "z", n, k).wait()

            def total(offset, n=n, size=size):
                value = grad_piece(n, chip * 2 * shard + offset, shard, False)[...].astype(F32)
                for k in range(1, depth):
                    _, row, col = stage_place(kind, "z", n, k)
                    value = value + gg[at(row + offset, shard), col : col + size].astype(F32)
                return value

            theirs = grad_piece(n, (i + 1 - 2 * core) * shard, shard, False)
            theirs[...] = total((1 - core) * shard).astype(BF16)
            c_copy_of(n).start()
            own[n * shard : (n + 1) * shard, 0:size] = total(core * shard)
            for c in out_copies(n, 0):
                c.start()

    def reduce_core(kind):
        for n in kind:
            lo, size = p.sum_segs[n]
            c_copy_of(n).wait_recv()
            mid_res[n * shard : (n + 1) * shard, 0:size] = cr[:, lo : lo + size].astype(F32)
            for c in out_copies(n, 1):
                c.start()

    def small_copy(n, k=0):
        device = (sib, over, aside)[n] if n < 3 else along(k)
        return remote(
            small_send.at[min(n, 3)], small_recv.at[n + max(k - 1, 0)],
            p.small + n + max(k - 1, 0), device,
        )

    def small_step(n):
        small_copy(n).wait_recv()
        small_send[n + 1] = small_send[n] + small_recv[n]

    for copies in core_sends[:2]:
        for c in copies:
            c.start()
    gain0, gain1 = gains[0:1, :], gains[1:2, :]
    x_copy.wait()
    for h in range(SPLIT):
        xf = ry_b[h * part : (h + 1) * part, :].astype(F32)
        rms = lax.rsqrt(jnp.mean(xf * xf, axis=1, keepdims=True) + epsilon)
        nfm[rows_of(core, y, h), :] = (xf * rms * gain0).astype(BF16)
        mid_res[h * part : (h + 1) * part, :] = xf
        tokens_send(nfm, p.t_first, h)
    gather_start(0)
    gather_start(1)
    for copies in core_sends[2:]:
        for c in copies:
            c.start()
    row = lax.broadcasted_iota(jnp.int32, (group, 128), 0)
    begun, start = jnp.zeros_like(row), 0
    for s in range(lengths.shape[1]):
        begun = jnp.where(row >= start, start, begun)
        start = start + lengths[0, s]
    for n in range(2):
        keep[core, :, 128 * n : 128 * (n + 1)] = jnp.where(
            row - begun >= n + 1, 1.0, 0.0
        ).astype(BF16)
    keep_send.start()
    small_send[...] = jnp.zeros_like(small_send)
    cot_local.wait()
    gather_forward(0)
    for h in range(SPLIT):
        tokens_send(cot, p.t_cot, h)
    gather_start(2)
    gather_forward(1)
    gather_done(0)

    def in_projection(step, carry):
        r = tokens_wait(nfm, p.t_first, step)
        proj[r, :] = dot_nn(nfm[r, :], w[:, 0 : 3 * p.cq]).astype(BF16)
        return carry

    lax.fori_loop(0, steps, in_projection, 0)
    tokens_sent(nfm, p.t_first)
    spill = local(nfm, spilled, p.l_spill)
    spill.start()
    hold = local(proj, proj_held, p.l_proj)
    hold.start()
    keep_send.wait_recv()
    gather_done(1)
    lanes = p.cq // 128

    def conv_terms(g, j):
        r = at(g * group, group)
        col = pl.multiple_of(j * 128, 128)
        b = proj[r, pl.ds(col, 128)].astype(F32)
        c = proj[r, pl.ds(pl.multiple_of(col + p.cq, 128), 128)].astype(F32)
        xv = proj[r, pl.ds(pl.multiple_of(col + 2 * p.cq, 128), 128)].astype(F32)
        k1 = keep[g, :, 0:128].astype(F32)
        k2 = keep[g, :, 128:256].astype(F32)
        t = taps_in[:, pl.ds(pl.multiple_of(core * p.cq + j * 128, 128), 128)]
        gated = b * xv
        d1 = pltpu.roll(gated, 1, 0) * k1
        d2 = pltpu.roll(gated, 2, 0) * k2
        conv = t[0:1] * gated + t[1:2] * d1 + t[2:3] * d2
        return r, col, b, c, xv, k1, k2, t, gated, d1, d2, conv

    def conv_forward(step, carry):
        g = jnp.where(step // lanes == 0, 1 - core, core)
        r, col, b, c, xv, k1, k2, t, gated, d1, d2, conv = conv_terms(g, step % lanes)
        mix[r, pl.ds(col, 128)] = (c * conv).astype(BF16)
        return carry

    lax.fori_loop(0, 2 * lanes, conv_forward, 0)

    def add_mid(r, value):
        mid_res[r, :] += value

    partials(
        p.u_out,
        lambda r: dot_nt(mix[r, :], w[:, 3 * p.cq : p.mix]),
        rd_a, sy_a, ry_a, add_mid,
    )
    spill.wait()
    for step in range(2 * SPLIT, 3 * SPLIT):
        tokens_wait(cot, p.t_cot, step)
    gather_forward(2)
    for s in range(3, min(4, len(p.gather_segs))):
        gather_start(s)
    for h in range(SPLIT):
        piece = slice(h * part, (h + 1) * part)
        over_copy(p.u_out, sy_a, ry_a, h).wait_recv()
        value = mid_res[piece, :] + ry_a[piece, :].astype(F32)
        mid_res[piece, :] = value
        rms = lax.rsqrt(jnp.mean(value * value, axis=1, keepdims=True) + epsilon)
        ns[rows_of(core, y, h), :] = (value * rms * gain1).astype(BF16)
        tokens_send(ns, p.t_second, h)
    for s in range(3, len(p.gather_segs)):
        if s == 3:
            gather_forward(s)
        else:
            gather_start(s)
    for step in list(range(SPLIT, 2 * SPLIT)) + list(range(3 * SPLIT, 4 * SPLIT)):
        tokens_wait(cot, p.t_cot, step)

    fc = p.fc

    def order(step):
        k = lax.rem(step + 1, depth)
        return k, lax.rem(z + k, depth) * 4 * shard

    def early_grads(step, carry):
        k, first = order(step)
        d = at(first, 4 * shard)
        grad_piece(0, first, 4 * shard)[...] = dot_tn(ns[:, d], gg[:, 0 : 2 * fc]).astype(BF16)
        x_copy_of(0, k).start()
        grad_piece(p.cuts, first, 4 * shard)[...] = dot_tn(cot[:, d], ha[:, 0:fc]).astype(BF16)
        x_copy_of(p.cuts, k).start()
        return carry

    def hidden(n):
        lo = p.gather_segs[2 + n][0]

        def step_of(step, carry):
            if n == 0:
                r = tokens_wait(ns, p.t_second, step)
            else:
                _, g, t, h = source(step)
                r = rows_of(g, t, h)
            gate = dot_nn(ns[r, :], w[:, lo : lo + fc])
            up = dot_nn(ns[r, :], w[:, lo + fc : lo + 2 * fc])
            act = dot_nn(cot[r, :], w[:, lo + 2 * fc : lo + 3 * fc])
            sig = 0.5 * jnp.tanh(0.5 * gate) + 0.5
            silu = gate * sig
            ha[r, n * fc : (n + 1) * fc] = (silu * up).astype(BF16)
            gg[r, 2 * n * fc : (2 * n + 1) * fc] = (
                act * up * (sig + silu * (1.0 - sig))
            ).astype(BF16)
            gg[r, (2 * n + 1) * fc : (2 * n + 2) * fc] = (act * silu).astype(BF16)
            return carry

        return step_of

    half = steps // 2
    gather_done(2)
    lax.fori_loop(0, half, hidden(0), 0)
    for n in range(1, p.cuts):
        if n > 1:
            gather_forward(2 + n)
        if n + 1 == p.cuts:
            lax.fori_loop(half, steps, hidden(0), 0)
            for m in range(1, n):
                lax.fori_loop(half, steps, hidden(m), 0)
            hold.wait()
            lax.fori_loop(0, depth, early_grads, 0)
            gather_done(2 + n)
            lax.fori_loop(0, steps, hidden(n), 0)
        else:
            gather_done(2 + n)
            lax.fori_loop(0, half, hidden(n), 0)
    tokens_sent(cot, p.t_cot)
    tokens_sent(ns, p.t_second)
    for s in range(len(p.gather_segs)):
        gather_sent(s)
    keep_send.wait_send()

    def gn2_product(r):
        value = None
        for n, (lo, size) in enumerate(p.gu_segs):
            term = dot_nt(gg[r, 2 * n * fc : (2 * n + 2) * fc], w[:, lo : lo + size])
            value = term if value is None else value + term
        return value

    def set_own(r, value):
        own[r, :] = value

    for h in range(SPLIT):
        over_copy(p.u_out, sy_a, ry_a, h).wait_send()
    partials(p.u_gn2, gn2_product, rd_a, sy_a, ry_a, set_own)

    for k in range(1, depth - 1):
        reduce_x(p.kind_early, k)

    def grad_gate_up(step, carry):
        k, first = order(step)
        d = at(first, 4 * shard)
        for n in p.kind_gu:
            lo, size = p.sum_segs[n]
            w[d, lo : lo + size] = dot_tn(
                ns[:, d], gg[:, 2 * n * fc : (2 * n + 2) * fc]
            ).astype(BF16)
            x_copy_of(n, k).start()
        return carry

    lax.fori_loop(0, depth, grad_gate_up, 0)
    for k in (depth - 1, 0):
        reduce_x(p.kind_early, k)
    for h in range(SPLIT):
        piece = slice(h * part, (h + 1) * part)
        over_copy(p.u_gn2, sy_a, ry_a, h).wait_recv()
        gn2 = own[piece, :] + ry_a[piece, :].astype(F32)
        res = mid_res[piece, :]
        rms = lax.rsqrt(jnp.mean(res * res, axis=1, keepdims=True) + epsilon)
        small_send[0, 1:2, :] += jnp.sum(gn2 * (res * rms), axis=0, keepdims=True)
        q = gn2 * gain1
        value = (
            cot[rows_of(core, y, h), :].astype(F32)
            + rms * q
            - res * (rms * rms * rms) * jnp.mean(q * res, axis=1, keepdims=True)
        )
        own[piece, :] = value
        nfm[rows_of(core, y, h), :] = value.astype(BF16)
        tokens_send(nfm, p.t_mid, h)

    reduce_x(p.kind_gu, 1)

    def blk_product(r):
        value = None
        for n, (lo, size) in enumerate(p.dn_segs):
            term = dot_nt(ha[r, n * fc : (n + 1) * fc], w[:, lo : lo + size])
            value = term if value is None else value + term
        return value

    for h in range(SPLIT):
        over_copy(p.u_gn2, sy_a, ry_a, h).wait_send()
    partials(p.u_blk, blk_product, rd_b, sy_a, ry_b, add_mid, hold=True)
    reduce_x(p.kind_gu, 2)
    restore = local(spilled, ns, p.l_spill)
    restore.start()
    def grad_down(step, carry):
        k, first = order(step)
        d = at(first, 4 * shard)
        for n in p.kind_dn:
            lo, size = p.sum_segs[n]
            first_unit = (n - p.cuts) * fc
            w[d, lo : lo + size] = dot_tn(
                cot[:, d], ha[:, first_unit : first_unit + fc]
            ).astype(BF16)
            x_copy_of(n, k).start()
        return carry

    lax.fori_loop(0, depth, grad_down, 0)
    for k in range(3, depth):
        reduce_x(p.kind_gu, k)

    grow = group
    gcol = p.cq

    def grad_mixer(step, carry):
        r = tokens_wait(nfm, p.t_mid, step)
        _, g, t, h = source(step)
        value = dot_nn(nfm[r, :], w[:, 3 * p.cq : p.mix]).astype(BF16)
        rr = at(grow + t * rows + h * part, part)

        @pl.when(g == 0)
        def _():
            gg[rr, 0:gcol] = value

        @pl.when(g == 1)
        def _():
            gg[rr, gcol : 2 * gcol] = value

        return carry

    lax.fori_loop(0, steps, grad_mixer, 0)
    for h in range(SPLIT):
        over_copy(p.u_blk, sy_a, ry_b, h).start()

    def conv_backward(step, carry):
        g = jnp.where(step // lanes == 0, 1 - core, core)
        j = step % lanes
        r, col, b, c, xv, k1, k2, t, gated, d1, d2, conv = conv_terms(g, j)
        gm = gg[grow : 2 * grow, pl.ds(pl.multiple_of(g * gcol + j * 128, 128), 128)].astype(F32)
        gco = gm * c
        grad_gated = (
            t[0:1] * gco
            + t[1:2] * pltpu.roll(gco * k1, group - 1, 0)
            + t[2:3] * pltpu.roll(gco * k2, group - 2, 0)
        )
        place = pl.ds(pl.multiple_of((y * 2 + core) * p.cq + j * 128, 128), 128)
        for n, term in enumerate((gated, d1, d2)):
            small_send[0, 8 + n : 9 + n, place] += jnp.sum(gco * term, axis=0, keepdims=True)
        proj[r, pl.ds(col, 128)] = (grad_gated * xv).astype(BF16)
        proj[r, pl.ds(pl.multiple_of(col + p.cq, 128), 128)] = (gm * conv).astype(BF16)
        proj[r, pl.ds(pl.multiple_of(col + 2 * p.cq, 128), 128)] = (grad_gated * b).astype(BF16)
        return carry

    for n in p.kind_early:
        first = chip * 2 * shard
        grad_piece(n, first, 2 * shard, False)[...] = grad_piece(n, first, 2 * shard)[...]
        for k in range(depth):
            x_copy_of(n, k).wait_send()
        for k in range(1, depth):
            z_copy_of(n, k).wait_send()
    proj_back = local(proj_held, proj, p.l_proj)
    proj_back.start()
    proj_back.wait()
    lax.fori_loop(0, 2 * lanes, conv_backward, 0)
    restore.wait()
    x_back = local(x_in, ha.at[rows:group, 0:width], p.l_x)
    x_back.start()
    mx0 = p.kind_mix[0]

    def grad_mix(step, carry):
        k, first = order(step)
        d = at(first, 4 * shard)
        place = at(group + first, 4 * shard)
        ha[place, 0 : 3 * p.cq] = dot_tn(ns[:, d], proj[...]).astype(BF16)
        ha[place, 3 * p.cq : p.mix] = dot_tn(nfm[:, d], mix[...]).astype(BF16)
        x_copy_of(mx0, k).start()
        return carry

    lax.fori_loop(0, depth, grad_mix, 0)
    reduce_x(p.kind_gu, 0)

    def block_output():
        for k in list(range(1, depth)) + [0]:
            reduce_x(p.kind_dn, k)
        for h in range(SPLIT):
            piece = slice(h * part, (h + 1) * part)
            over_copy(p.u_blk, sy_a, ry_b, h).wait_recv()
            ha[piece, 0:width] = (mid_res[piece, :] + ry_b[piece, :].astype(F32)).astype(BF16)
        local(ha.at[0:rows, 0:width], blk_out, p.l_blk).start()

    def gain_sum(r, value):
        small_send[0, 0:1, :] += jnp.sum(value * ns[r, :].astype(F32), axis=0, keepdims=True)

    def set_mid(r, value):
        mid_res[r, :] = value

    partials(
        p.u_gn1,
        lambda r: dot_nt(proj[r, :], w[:, 0 : 3 * p.cq]),
        rd_a, rd_b, ry_a, set_mid, between=block_output, observe=gain_sum,
    )
    small_copy(0).start()
    reduce_x(p.kind_mix, 1)
    small_step(0)
    small_copy(1).start()
    reduce_x(p.kind_mix, 2)
    small_step(1)
    small_copy(2).start()
    for k in list(range(3, depth)) + [0]:
        reduce_x(p.kind_mix, k)
    small_step(2)
    for k in range(1, depth):
        small_copy(3, k).start()
    x_back.wait()
    for h in range(SPLIT):
        piece = slice(h * part, (h + 1) * part)
        over_copy(p.u_gn1, rd_b, ry_a, h).wait_recv()
        gn1 = mid_res[piece, :] + ry_a[piece, :].astype(F32)
        xf = ha[rows + h * part : rows + (h + 1) * part, 0:width].astype(F32)
        rms = lax.rsqrt(jnp.mean(xf * xf, axis=1, keepdims=True) + epsilon)
        q = gn1 * gain0
        if h == 0:
            local(ha.at[0:rows, 0:width], blk_out, p.l_blk).wait()
        ha[piece, 0:width] = (
            own[piece, :]
            + rms * q
            - xf * (rms * rms * rms) * jnp.mean(q * xf, axis=1, keepdims=True)
        ).astype(BF16)
    tok_copy = local(ha.at[0:rows, 0:width], tok_out, p.l_tok)
    tok_copy.start()

    reduce_z(p.kind_early)
    reduce_z(p.kind_gu)
    reduce_core(p.kind_early)
    reduce_z(p.kind_dn)
    reduce_core(p.kind_gu)
    reduce_z(p.kind_mix)
    reduce_core(p.kind_dn)
    total = small_send[3]
    for k in range(1, depth):
        small_copy(3, k).wait_recv()
        total = total + small_recv[3 + k - 1]
    small_recv[2] = total
    half_chan = 2 * p.cq
    taps_out[...] = small_recv[2, 8:11, pl.ds(pl.multiple_of(y * half_chan, 128), half_chan)]
    sums_out[0:1, :] = total[0:1, :] / gain0
    sums_out[1:2, :] = total[1:2, :]
    reduce_core(p.kind_mix)
    for n in range(len(p.sum_segs)):
        for c in out_copies(n, 0) + out_copies(n, 1):
            c.wait()
    tok_copy.wait()
    for h in range(SPLIT):
        over_copy(p.u_blk, sy_a, ry_b, h).wait_send()
    tokens_sent(nfm, p.t_mid)
    for h in range(SPLIT):
        over_copy(p.u_gn1, rd_b, ry_a, h).wait_send()
    for n in range(len(p.sum_segs)):
        if n not in p.kind_early:
            for k in range(depth):
                x_copy_of(n, k).wait_send()
            for k in range(1, depth):
                z_copy_of(n, k).wait_send()
        c_copy_of(n).wait_send()
    for n in range(3):
        small_copy(n).wait_send()
    for k in range(1, depth):
        small_copy(3, k).wait_send()


def fused_body(depth, tokens, cotangent, lengths, w_in, w_out, w_gate_up, w_down, conv_weight, norm_gains):
    rows, width = tokens.shape
    shard, taken, chan = w_in.shape
    hidden = w_gate_up.shape[2]
    plan = Plan(depth, rows, width, shard, chan, hidden)
    if plan.cuts < 3 or plan.width > 2 * rows or (2 * plan.cuts + 1) * shard > rows:
        return body(
            tokens, cotangent, lengths, w_in, w_out, w_gate_up, w_down, conv_weight, norm_gains
        )
    cq = plan.cq
    total = 4 * rows
    any_spec = pl.BlockSpec(memory_space=pl.ANY)
    vmem_spec = pl.BlockSpec(memory_space=pltpu.VMEM)
    shape = jax.ShapeDtypeStruct
    outs = (
        shape((rows, width), BF16),
        shape((rows, width), BF16),
        shape((taken, shard, chan), F32),
        shape((shard, chan), F32),
        shape((2, shard, hidden), F32),
        shape((shard, hidden), F32),
        shape(conv_weight.shape, F32),
        shape((2, width), F32),
        shape((depth, 2 * shard, plan.cols), BF16),
        shape((depth - 1, 2 * shard, plan.cols), BF16),
        shape((total, width), BF16),
        shape((total, 3 * cq), BF16),
    )
    vm = pltpu.VMEM
    block_out, grad_tokens, grad_in, grad_out, grad_gu, grad_dn, grad_taps, sums, _, _, _, _ = pl.pallas_call(
        functools.partial(block_kernel, plan),
        out_shape=outs,
        in_specs=[
            any_spec, any_spec, pl.BlockSpec(memory_space=pltpu.SMEM),
            any_spec, any_spec, any_spec, any_spec, vmem_spec, vmem_spec,
        ],
        out_specs=(any_spec,) * 6 + (vmem_spec,) * 2 + (any_spec,) * 4,
        scratch_shapes=[
            vm((width, plan.cols), BF16),
            vm((total, width), BF16),
            vm((total, width), BF16),
            vm((total, width), BF16),
            vm((total, 3 * cq), BF16),
            vm((total, 2 * plan.fq), BF16),
            vm((total, plan.fq), BF16),
            vm((total, cq), BF16),
            vm((2 * rows, width), BF16),
            vm((2 * rows, width), BF16),
            vm((rows, width), BF16),
            vm((rows, width), BF16),
            vm((2 * rows, width), BF16),
            vm((rows, width), BF16),
            vm((rows, width), F32),
            vm((rows, width), F32),
            vm((shard, plan.cols), BF16),
            vm((2, 2 * rows, 256), BF16),
            vm((4, 16, width), F32),
            vm((3 + depth - 1, 16, width), F32),
            pltpu.SemaphoreType.DMA((plan.remote,)),
            pltpu.SemaphoreType.DMA((plan.remote,)),
            pltpu.SemaphoreType.DMA((plan.local,)),
        ],
        compiler_params=pltpu.CompilerParams(
            collective_id=0, has_side_effects=True, vmem_limit_bytes=63 * 2**20
        ),
    )(
        tokens, cotangent, lengths, w_in.transpose(1, 0, 2), w_out.T, w_gate_up.transpose(1, 0, 2),
        w_down.T, conv_weight, norm_gains,
    )
    return (
        block_out,
        grad_tokens,
        grad_in.transpose(1, 0, 2),
        grad_out.T,
        grad_gu.transpose(1, 0, 2),
        grad_dn.T,
        grad_taps,
        sums,
    )


def solution(mesh):
    dp, tensor = mesh.shape["dp"], mesh.shape["tensor"]
    grouped = tensor == 2 and dp == 16
    return jax.shard_map(
        functools.partial(fused_body, dp // 4) if grouped else body,
        mesh=mesh,
        in_specs=(
            P(("dp", "tensor"), None),
            P(("dp", "tensor"), None),
            P("dp", None),
            P("dp", None, "tensor"),
            P("tensor", "dp"),
            P("dp", None, "tensor"),
            P("tensor", "dp"),
            P(None, "tensor"),
            P(),
        ),
        out_specs=(
            P(("dp", "tensor"), None),
            P(("dp", "tensor"), None),
            P("dp", None, "tensor"),
            P("tensor", "dp"),
            P("dp", None, "tensor"),
            P("tensor", "dp"),
            P(None, "tensor"),
            P(),
        ),
        check_vma=False,
    )
```
